256 devices in a mesh: depth: 32 (over y, x, core), rows: 8 (over z).
Axes of the slice: x: 4, y: 4, z: 8, core: 2. Of those that a mesh axis runs over, the one named last changes fastest.
Arguments:
- initial: float32 [32, 256, 128], P('rows'), may hold values from -6 to 6
- forward_guess: float32 [64, 32, 256, 128], P('depth', 'rows'), may hold values from -6 to 6
- adjoint_guess: float32 [64, 32, 256, 128], P('depth', 'rows'), may hold values from -6 to 6
- cotangent: float32 [32, 256, 128], P('rows'), may hold values from -6 to 6
- kernel: bfloat16 [3, 3, 128, 128], replicated, may hold values from -0.125 to 0.125
- conv_bias: float32 [128], replicated, may hold values from -1.5 to 1.5
Outputs:
- states: float32 [64, 32, 256, 128], P('depth', 'rows')
- adjoints: float32 [64, 32, 256, 128], P('depth', 'rows')
- grad_kernel: float32 [3, 3, 128, 128], replicated
- grad_bias: float32 [128], replicated
The draws below stay inside these ranges and needn't reach their ends.
All inputs are finite; a program needn't handle non-finite values.
Results may differ from the reference program's by a relative error of at most 0.0025.
The reference program's roundings to bfloat16 on the way count: a program that leaves them out, or rounds other values in their place, can miss the bound.
Values may be sent and summed in bfloat16 or wider, within the bound.
No kernel may reach another device: no remote copies, remote signals or barrier semaphores. Data moves between devices by JAX's collectives and lax.ppermute only.
A program may use at most 64 MiB of HBM per device.

```python
import jax
import jax.numpy as jnp
from jax import lax

C = 128
W = 256
H = 32
STEPS = 64


def level_of(key, dims, split, least, high):
    gain, own = 1.0, jax.random.fold_in(key, 6)
    for position, shards_of in split:
        steps = jnp.exp(jax.random.uniform(jax.random.fold_in(own, position), (shards_of,), jnp.float32, least / len(split), high / len(split)))
        gain = gain * jnp.repeat(steps, dims[position] // shards_of).reshape([-1 if axis == position else 1 for axis in range(len(dims))])
    return gain


def normal_values(key, shape, scale, reach, cuts=(), held_as=jnp.bfloat16):
    factor_of = level_of(key, shape, cuts, -0.22, 0.18) if cuts else 1.0
    drawn = jax.random.normal(key, shape, jnp.float32) * scale * factor_of
    return jnp.minimum(jnp.maximum(drawn, -reach), reach).astype(held_as)


def setup_inputs(seed: int = 0) -> dict:
    keys = jax.random.split(jax.random.key(seed), 7)
    return {
        "initial": normal_values(keys[0], (H, W, C), 1.0, 6.0, ((0, 8),), jnp.float32),
        "forward_guess": normal_values(keys[1], (STEPS, H, W, C), 1.0, 6.0, ((0, 32), (1, 8)), jnp.float32),
        "adjoint_guess": normal_values(keys[2], (STEPS, H, W, C), 1.0, 6.0, ((0, 32), (1, 8)), jnp.float32),
        "cotangent": normal_values(keys[3], (H, W, C), 1.0, 6.0, ((0, 8),), jnp.float32),
        "kernel": normal_values(keys[4], (3, 3, C, C), (18 * C) ** -0.5, 0.125),
        "conv_bias": normal_values(keys[5], (C,), 0.3, 1.5, (), jnp.float32),
    }


STEP_SIZE = 0.2


def restrict(signal):
    row_count, col_count, channels = signal.shape
    return signal.reshape(row_count // 2, 2, col_count // 2, 2, channels).mean(axis=(1, 3))


def prolong(signal):
    return jnp.repeat(jnp.repeat(signal, 2, axis=0), 2, axis=1)


def taps_product(padded, kernel, row_count, col_count):
    summed = jnp.zeros((row_count * col_count, kernel.shape[3]), jnp.float32)
    for row_tap in range(3):
        for col_tap in range(3):
            window = padded[row_tap:row_tap + row_count, col_tap:col_tap + col_count].reshape(row_count * col_count, -1)
            summed = summed + jnp.dot(window, kernel[row_tap, col_tap], preferred_element_type=jnp.float32)
    return summed.reshape(row_count, col_count, -1)


def surround(signal):
    return jnp.pad(signal, ((1, 1), (1, 1), (0, 0)))


def advance(current, kernel, conv_bias, on_coarse):
    factor = 2.0 * STEP_SIZE if on_coarse else STEP_SIZE
    squashed = jnp.tanh(current).astype(jnp.bfloat16)
    padded = surround(squashed)
    return current + factor * (taps_product(padded, kernel, current.shape[0], current.shape[1]) + conv_bias)


def retreat(current, adjoint, kernel_flip, on_coarse):
    factor = 2.0 * STEP_SIZE if on_coarse else STEP_SIZE
    derivative = 1.0 - jnp.tanh(current) ** 2
    padded = surround(adjoint.astype(jnp.bfloat16))
    return adjoint + factor * derivative * taps_product(padded, kernel_flip, adjoint.shape[0], adjoint.shape[1])


def kernel_terms(padded, cotan, row_count, col_count):
    flat = cotan.reshape(row_count * col_count, -1)
    tap_rows = []
    for row_tap in range(3):
        tap_cols = []
        for col_tap in range(3):
            window = padded[row_tap:row_tap + row_count, col_tap:col_tap + col_count].reshape(row_count * col_count, -1)
            tap_cols.append(lax.dot_general(window, flat, (((0,), (0,)), ((), ())), preferred_element_type=jnp.float32))
        tap_rows.append(jnp.stack(tap_cols))
    return jnp.stack(tap_rows)


def reference(initial, forward_guess, adjoint_guess, cotangent, kernel, conv_bias):
    n_steps = forward_guess.shape[0]
    half_count = n_steps // 2
    row_count, col_count = initial.shape[0], initial.shape[1]
    kernel_flip = jnp.transpose(jnp.flip(kernel, (0, 1)), (0, 1, 3, 2))
    guesses = [initial] + [forward_guess[n] for n in range(n_steps)]
    relaxed = [initial]
    for n in range(1, n_steps + 1):
        if n % 2 == 1:
            relaxed.append(advance(guesses[n - 1], kernel, conv_bias, False))
        else:
            relaxed.append(guesses[n])
    solution = restrict(initial)
    coarse_states = [solution]
    corrected = list(relaxed)
    for k in range(1, half_count + 1):
        rhs_here = restrict(advance(relaxed[2 * k - 1], kernel, conv_bias, False)) - advance(restrict(relaxed[2 * k - 2]), kernel, conv_bias, True)
        solution = advance(solution, kernel, conv_bias, True) + rhs_here
        coarse_states.append(solution)
        corrected[2 * k] = relaxed[2 * k] + prolong(solution - restrict(relaxed[2 * k]))
    fine_states = [initial]
    for n in range(1, n_steps + 1):
        if n % 2 == 1:
            fine_states.append(advance(corrected[n - 1], kernel, conv_bias, False))
        else:
            fine_states.append(corrected[n])
    targets = [adjoint_guess[n] for n in range(n_steps)] + [cotangent]
    primal = []
    for n in range(n_steps):
        if n % 2 == 1:
            primal.append(retreat(fine_states[n], targets[n + 1], kernel_flip, False))
        else:
            primal.append(targets[n])
    primal.append(cotangent)
    fixed = list(primal)
    correction = jnp.zeros_like(restrict(initial))
    for k in range(half_count - 1, -1, -1):
        residual = retreat(fine_states[2 * k], primal[2 * k + 1], kernel_flip, False) - primal[2 * k]
        correction = retreat(coarse_states[k], correction, kernel_flip, True) + restrict(residual)
        fixed[2 * k] = primal[2 * k] + prolong(correction)
    lambdas = []
    for n in range(n_steps):
        if n % 2 == 1:
            lambdas.append(retreat(fine_states[n], fixed[n + 1], kernel_flip, False))
        else:
            lambdas.append(fixed[n])
    lambdas.append(cotangent)
    grad_sum = jnp.zeros(kernel.shape, jnp.float32)
    bias_sum = jnp.zeros((kernel.shape[3],), jnp.float32)
    for n in range(n_steps):
        squashed = jnp.tanh(fine_states[n]).astype(jnp.bfloat16)
        grad_sum = grad_sum + kernel_terms(surround(squashed), lambdas[n + 1].astype(jnp.bfloat16), row_count, col_count)
        bias_sum = bias_sum + jnp.sum(lambdas[n + 1], axis=(0, 1))
    factor = STEP_SIZE / (row_count * col_count)
    states = jnp.stack(fine_states[1:])
    adjoints = jnp.stack(lambdas[:n_steps])
    return states, adjoints, grad_sum * factor, bias_sum * factor
```

```python
import functools

import jax
import jax.numpy as jnp
from jax import lax
from jax.experimental import pallas as pl
from jax.experimental.pallas import tpu as pltpu
from jax.sharding import Mesh, PartitionSpec as P

STEP_SIZE = 0.2
COARSE_SIZE = 2.0 * STEP_SIZE
GROUPS = 1
AXES = ("group", "member", "rows")
CHANNELS = 128
SMEM = pl.BlockSpec(memory_space=pltpu.SMEM)
VMEM = pl.BlockSpec(memory_space=pltpu.VMEM)
PARAMS = pltpu.CompilerParams(vmem_limit_bytes=60 * 1024 * 1024)


def shape_of(*dims, dtype=jnp.float32):
    return jax.ShapeDtypeStruct(dims, dtype)


def spread(even, odd, width):
    count = even.shape[0]
    place = lax.broadcasted_iota(jnp.int32, even.shape, 0) % width
    before = jnp.where(place == 0, 0.0, pltpu.roll(odd, 1, 0))
    after = jnp.where(place == width - 1, 0.0, pltpu.roll(even, count - 1, 0))
    return jnp.concatenate([even, odd, before, after], axis=1).astype(jnp.bfloat16)


def taps(ref, start, count, width, weights):
    lhs = jnp.concatenate(
        [ref[start + tap * width : start + tap * width + count] for tap in range(3)], axis=1
    )
    return jnp.dot(lhs, weights, preferred_element_type=jnp.float32)


def halves(value):
    return value[:, :CHANNELS], value[:, CHANNELS:]


def pair_weights(kernel):
    none = jnp.zeros_like(kernel[:, 0])
    left, mid, right = kernel[:, 0], kernel[:, 1], kernel[:, 2]
    to_even = jnp.concatenate([mid, right, left, none], axis=1)
    to_odd = jnp.concatenate([left, mid, none, right], axis=1)
    return jnp.concatenate([to_even, to_odd], axis=2).reshape(12 * CHANNELS, 2 * CHANNELS)


def row_planes(ref, row, cols):
    return ref[row, pl.ds(0, cols // 2, stride=2), :], ref[row, pl.ds(1, cols // 2, stride=2), :]


def planes_of(refs_rows, cols):
    pairs = [row_planes(ref, row, cols) for ref, row in refs_rows]
    return jnp.concatenate([e for e, _ in pairs], 0), jnp.concatenate([o for _, o in pairs], 0)


def with_halo(top, main, bottom, halo):
    rows = [(top, 2 - halo + i) for i in range(halo)]
    rows += [(main, i) for i in range(main.shape[0])]
    return rows + [(bottom, i) for i in range(halo)]


def restricted(even, odd, pairs):
    both = even + odd
    return [
        (both[i * pairs : (i + 1) * pairs] + both[(i + 1) * pairs : (i + 2) * pairs]) * 0.25
        for i in range(0, both.shape[0] // pairs, 2)
    ]


def masked(value, pairs, at_top, at_bottom):
    count = value.shape[0] // pairs
    parts = [value[i * pairs : (i + 1) * pairs] for i in range(count)]
    parts[0] = jnp.where(at_top, jnp.zeros_like(parts[0]), parts[0])
    parts[-1] = jnp.where(at_bottom, jnp.zeros_like(parts[-1]), parts[-1])
    return jnp.concatenate(parts, 0)


def store_planes(out, scratch, rows, pairs):
    half = pairs // 2
    for i, row in enumerate(rows):
        scratch[...] = row
        for plane in range(2):
            base = (plane * len(rows) + i) * half
            out[base : base + half] = scratch[pl.ds(plane, half, stride=2), :]


def natural_rows(ref, scratch, count, pairs):
    half = pairs // 2
    rows = []
    for i in range(count):
        for plane in range(2):
            scratch[i, pl.ds(plane, half, stride=2), :] = ref[plane, i * half : (i + 1) * half]
        rows.append(scratch[i])
    return rows


def relax_kernel(
    shards_z, meta, top, main, bottom, first, weights, plain, bias, sent, fine, coarse, row, start
):
    pairs = main.shape[1] // 2
    at_top, at_bottom = meta[0] == 0, meta[0] == shards_z - 1
    even, odd = planes_of(with_halo(top, main, bottom, 2), main.shape[1])
    fine[...] = spread(jnp.tanh(even), jnp.tanh(odd), pairs)
    six = slice(pairs, 7 * pairs)
    conv_even, conv_odd = halves(taps(fine, 0, 6 * pairs, pairs, weights[...]))
    odd_even = masked(even[six] + STEP_SIZE * (conv_even + bias[...]), pairs, at_top, at_bottom)
    odd_odd = masked(odd[six] + STEP_SIZE * (conv_odd + bias[...]), pairs, at_top, at_bottom)
    fine[0 : 6 * pairs] = spread(jnp.tanh(odd_even), jnp.tanh(odd_odd), pairs)
    conv_even, conv_odd = halves(taps(fine, 0, 4 * pairs, pairs, weights[...]))
    four = slice(pairs, 5 * pairs)
    two_even = odd_even[four] + STEP_SIZE * (conv_even + bias[...])
    two_odd = odd_odd[four] + STEP_SIZE * (conv_odd + bias[...])
    fine_rows = restricted(two_even, two_odd, pairs)
    own = restricted(even, odd, pairs)
    place = lax.broadcasted_iota(jnp.int32, own[0].shape, 0)
    for i, value in enumerate(own):
        squashed = jnp.tanh(value)
        before = jnp.where(place == 0, 0.0, pltpu.roll(squashed, 1, 0))
        after = jnp.where(place == pairs - 1, 0.0, pltpu.roll(squashed, pairs - 1, 0))
        coarse[i * pairs : (i + 1) * pairs] = jnp.concatenate([before, squashed, after], 1).astype(
            jnp.bfloat16
        )
    conv = taps(coarse, 0, 2 * pairs, pairs, plain[...])
    rows = [
        fine_rows[i]
        - (own[i + 1] + COARSE_SIZE * (conv[i * pairs : (i + 1) * pairs] + bias[...]))
        for i in range(2)
    ]
    store_planes(sent, row, rows, pairs)
    even, odd = planes_of([(first, i) for i in range(4)], first.shape[1])
    store_planes(start, row, restricted(even, odd, pairs), pairs)
    share = sent.shape[0] - start.shape[0]
    sent[start.shape[0] :] = start[pl.ds(pl.multiple_of(meta[1] * share, share), share)]


def chain_kernel(forward, opening, closing, shards_z, meta, initial, *refs):
    received, refs = (None, refs) if opening else (refs[0], refs[1:])
    step, turns = pl.program_id(0), pl.num_programs(0)
    pos, member, edge = meta[0], meta[1], meta[2]
    if forward:
        terms, weights, bias, leaving, *outs, state, taps_in = refs
    else:
        slopes, terms, weights, leaving, *outs, state, taps_in = refs
    slab = initial.shape[2]
    half = slab // 2
    cells = shards_z * slab

    @pl.when(step == 0)
    def _():
        for plane in range(2):
            state[plane, 0:half] = jnp.zeros((half, CHANNELS), jnp.float32)
            state[plane, half + cells : 2 * half + cells] = jnp.zeros((half, CHANNELS), jnp.float32)
        taps_in[0:half] = jnp.zeros((half, 4 * CHANNELS), jnp.bfloat16)
        taps_in[half + cells : 2 * half + cells] = jnp.zeros((half, 4 * CHANNELS), jnp.bfloat16)
        for turn in range(shards_z):
            place = pl.ds(pl.multiple_of(half + lax.rem(pos + turn, shards_z) * slab, half), slab)
            value = initial[turn] if forward else jnp.zeros((2, slab, CHANNELS), jnp.float32)
            if not opening:
                value = jnp.where(edge == 1, value, received[turn])
            state[:, place] = value

    own = pl.ds(pl.multiple_of(half + pos * slab, half), slab)
    around = pl.ds(pl.multiple_of(pos * slab, half), 2 * slab)
    mine = member if forward else turns - 1 - member
    if closing:

        @pl.when(step == mine)
        def _():
            outs[0][...] = state[:, around]

    chunk = 2 * slab
    for i in range(cells // chunk):
        span = slice(half + i * chunk, half + (i + 1) * chunk)
        even, odd = state[0, span], state[1, span]
        if forward:
            even, odd = jnp.tanh(even), jnp.tanh(odd)
            if closing:
                @pl.when(step < turns - 1)
                def _(even=even, odd=odd, i=i):
                    outs[2][0, 0, i * chunk : (i + 1) * chunk] = COARSE_SIZE * (1.0 - even * even)
                    outs[2][0, 1, i * chunk : (i + 1) * chunk] = COARSE_SIZE * (1.0 - odd * odd)

        taps_in[span] = spread(even, odd, half)
    for turn in range(shards_z):
        place = pl.ds(pl.multiple_of(half + lax.rem(pos + turn, shards_z) * slab, half), slab)
        for plane in range(2):
            state[plane, place] += terms[0, turn, plane * slab : (plane + 1) * slab]
    for i in range(cells // chunk):
        conv = taps(taps_in, i * chunk, chunk, half, weights[...])
        for j in range(2):
            part = halves(conv[j * slab : (j + 1) * slab])
            span = slice(half + (2 * i + j) * slab, half + (2 * i + j + 1) * slab)
            for plane in range(2):
                if forward:
                    moved = COARSE_SIZE * (part[plane] + bias[...])
                else:
                    rows = slice((2 * i + j) * slab, (2 * i + j + 1) * slab)
                    moved = slopes[0, plane, rows] * part[plane]
                state[plane, span] += moved
    if closing:

        @pl.when(step == mine)
        def _():
            outs[1][...] = state[:, own]

    @pl.when(step == turns - 1)
    def _():
        leaving[...] = state[:, own]


def correct_kernel(
    shards_z,
    meta,
    top,
    main,
    bottom,
    guess,
    ahead_top,
    ahead_main,
    ahead_bottom,
    target,
    before_slab,
    own_slab,
    weights,
    flipped,
    bias,
    states,
    residual,
    even_taps,
    odd_taps,
    odd_slope,
    fine,
    natural,
    row,
):
    cols = main.shape[1]
    pairs = cols // 2
    at_top, at_bottom = meta[0] == 0, meta[0] == shards_z - 1
    even, odd = planes_of(with_halo(top, main, bottom, 2), cols)
    rest = restricted(even, odd, pairs)
    found = natural_rows(before_slab, natural, 4, pairs)
    change = [jnp.where(meta[3] == 1, 0.0, a - b) for a, b in zip(found, rest)]
    change = jnp.concatenate([c for c in change for _ in range(2)], 0)
    even, odd = even + change, odd + change

    here, there = planes_of([(guess, i) for i in range(4)], cols)
    rest = restricted(here, there, pairs)
    found = natural_rows(own_slab, natural, 2, pairs)
    change = jnp.concatenate([a - b for a, b in zip(found, rest) for _ in range(2)], 0)
    here, there = here + change, there + change
    for i in range(4):
        span = slice(i * pairs, (i + 1) * pairs)
        states[1, i, pl.ds(0, pairs, stride=2), :] = here[span]
        states[1, i, pl.ds(1, pairs, stride=2), :] = there[span]

    tanh_even, tanh_odd = jnp.tanh(even), jnp.tanh(odd)
    fine[...] = spread(tanh_even, tanh_odd, pairs)
    six, four = slice(pairs, 7 * pairs), slice(pairs, 5 * pairs)
    even_taps[...] = fine[six]
    own = slice(2 * pairs, 6 * pairs)
    slope_even = STEP_SIZE * (1.0 - tanh_even[own] ** 2)
    slope_odd = STEP_SIZE * (1.0 - tanh_odd[own] ** 2)
    conv_even, conv_odd = halves(taps(fine, 0, 6 * pairs, pairs, weights[...]))
    even = masked(even[six] + STEP_SIZE * (conv_even + bias[...]), pairs, at_top, at_bottom)
    odd = masked(odd[six] + STEP_SIZE * (conv_odd + bias[...]), pairs, at_top, at_bottom)
    for i in range(4):
        span = slice((i + 1) * pairs, (i + 2) * pairs)
        states[0, i, pl.ds(0, pairs, stride=2), :] = even[span]
        states[0, i, pl.ds(1, pairs, stride=2), :] = odd[span]
    tanh_even, tanh_odd = jnp.tanh(even), jnp.tanh(odd)
    odd_taps[...] = spread(tanh_even, tanh_odd, pairs)
    step_even, step_odd = STEP_SIZE * (1.0 - tanh_even**2), STEP_SIZE * (1.0 - tanh_odd**2)
    odd_slope[0] = step_even[four]
    odd_slope[1] = step_odd[four]

    even, odd = planes_of(with_halo(ahead_top, ahead_main, ahead_bottom, 2), cols)
    fine[...] = spread(even, odd, pairs)
    conv_even, conv_odd = halves(taps(fine, 0, 6 * pairs, pairs, flipped[...]))
    even = masked(even[six] + step_even * conv_even, pairs, at_top, at_bottom)
    odd = masked(odd[six] + step_odd * conv_odd, pairs, at_top, at_bottom)
    fine[0 : 6 * pairs] = spread(even, odd, pairs)
    conv_even, conv_odd = halves(taps(fine, 0, 4 * pairs, pairs, flipped[...]))
    here, there = planes_of([(target, i) for i in range(4)], cols)
    even = even[four] + slope_even * conv_even - here
    odd = odd[four] + slope_odd * conv_odd - there
    store_planes(residual, row, restricted(even, odd, pairs), pairs)


def finish_kernel(
    scale,
    top,
    main,
    bottom,
    target,
    ahead_slab,
    own_slab,
    even_taps,
    odd_taps,
    odd_slope,
    flipped,
    adjoints,
    grads,
    fine,
    natural,
):
    cols = main.shape[1]
    pairs = cols // 2
    here, there = planes_of([(target, i) for i in range(4)], cols)
    change = natural_rows(own_slab, natural, 2, pairs)
    change = jnp.concatenate([c for c in change for _ in range(2)], 0)
    here, there = here + change, there + change
    for i in range(4):
        span = slice(i * pairs, (i + 1) * pairs)
        adjoints[0, i, pl.ds(0, pairs, stride=2), :] = here[span]
        adjoints[0, i, pl.ds(1, pairs, stride=2), :] = there[span]
    even, odd = planes_of(with_halo(top, main, bottom, 1), cols)
    found = natural_rows(ahead_slab, natural, 4, pairs)
    change = jnp.concatenate([found[0], found[1], found[1], found[2], found[2], found[3]], 0)
    even, odd = even + change, odd + change
    fine[...] = spread(even, odd, pairs)
    conv_even, conv_odd = halves(taps(fine, 0, 4 * pairs, pairs, flipped[...]))
    four = slice(pairs, 5 * pairs)
    even, odd = even[four], odd[four]
    new_even, new_odd = even + odd_slope[0] * conv_even, odd + odd_slope[1] * conv_odd
    for i in range(4):
        span = slice(i * pairs, (i + 1) * pairs)
        adjoints[1, i, pl.ds(0, pairs, stride=2), :] = new_even[span]
        adjoints[1, i, pl.ds(1, pairs, stride=2), :] = new_odd[span]
    right = jnp.concatenate(
        [
            jnp.concatenate([new_even, new_odd], 1).astype(jnp.bfloat16),
            jnp.concatenate([even, odd], 1).astype(jnp.bfloat16),
        ],
        0,
    )
    one, two, three, four_ = (slice(i * CHANNELS, (i + 1) * CHANNELS) for i in range(4))
    for tap in range(3):
        span = slice(tap * pairs, (tap + 4) * pairs)
        left = jnp.concatenate([even_taps[span], odd_taps[span]], 0)
        found = lax.dot_general(
            left, right, (((0,), (0,)), ((), ())), preferred_element_type=jnp.float32
        )
        base = tap * 3 * CHANNELS
        grads[base : base + CHANNELS] = scale * (found[one, two] + found[three, one])
        grads[base + CHANNELS : base + 2 * CHANNELS] = scale * (found[one, one] + found[two, two])
        grads[base + 2 * CHANNELS : base + 3 * CHANNELS] = scale * (
            found[two, one] + found[four_, two]
        )
    total = jnp.sum(new_even + new_odd + even + odd, axis=0, keepdims=True)
    base = 9 * CHANNELS
    rest = grads.shape[0] - base
    place = lax.broadcasted_iota(jnp.int32, (rest, CHANNELS), 0)
    grads[base:] = jnp.where(place == 0, scale * total, 0.0)


def shards(initial, forward_guess, adjoint_guess, cotangent, kernel, conv_bias):
    groups, members, zs = (lax.axis_size(axis) for axis in AXES)
    depth = groups * members
    group, member, pos = (lax.axis_index(axis) for axis in AXES)
    index = group * members + member
    at_first, at_last = index == 0, index == depth - 1
    row_count, cols, _ = initial.shape
    pairs = cols // 2
    slab = 2 * pairs // 2
    cells = zs * slab
    bias = conv_bias.reshape(1, CHANNELS)
    meta = jnp.stack(
        [pos, member, (group == 0).astype(jnp.int32), at_first.astype(jnp.int32)]
    ).astype(jnp.int32)
    back_meta = jnp.stack(
        [pos, member, (group == groups - 1).astype(jnp.int32), at_last.astype(jnp.int32)]
    ).astype(jnp.int32)

    def moved(value, along, across):
        pairs_ = [
            (d * zs + z, (d + along) % depth * zs + z + across)
            for d in range(depth)
            for z in range(zs)
            if 0 <= z + across < zs
        ]
        return lax.ppermute(value, AXES, pairs_)

    def around(value, along):
        value_top = moved(value[row_count - 2 :], along, 1)
        value_bottom = moved(value[:2], along, -1)
        return value_top, moved(value, along, 0), value_bottom

    before = around(jnp.where(at_last, initial, forward_guess[1]), 1)
    ahead = around(jnp.where(at_first, cotangent, adjoint_guess[0]), -1)

    weights = pair_weights(kernel)
    plain = kernel.reshape(9 * CHANNELS, CHANNELS)
    flipped = pair_weights(jnp.transpose(jnp.flip(kernel, (0, 1)), (0, 1, 3, 2)))

    share = 2 * slab // depth
    sent = pl.pallas_call(
        functools.partial(relax_kernel, zs),
        out_shape=shape_of(2 * slab + share, CHANNELS),
        in_specs=[SMEM] + [VMEM] * 7,
        out_specs=VMEM,
        scratch_shapes=[
            pltpu.VMEM((8 * pairs, 4 * CHANNELS), jnp.bfloat16),
            pltpu.VMEM((4 * pairs, 3 * CHANNELS), jnp.bfloat16),
            pltpu.VMEM((pairs, CHANNELS), jnp.float32),
            pltpu.VMEM((2 * slab, CHANNELS), jnp.float32),
        ],
        compiler_params=PARAMS,
        name="relax",
    )(meta, *before, initial, weights, plain, bias)

    def over_rows(value):
        ring = [
            lax.ppermute(value, "rows", [((i + turn) % zs, i) for i in range(zs)])
            for turn in range(1, zs)
        ]
        return jnp.stack([value] + ring)

    def over_members(value):
        return lax.all_gather(over_rows(value.astype(jnp.float16)), "member")

    def passed(value, along):
        ring = []
        for turn in range(zs):
            pairs_ = [
                ((g * members + m) * zs + (z + turn) % zs, ((g + along) * members + m) * zs + z)
                for g in range(groups)
                if 0 <= g + along < groups
                for m in range(members)
                for z in range(zs)
            ]
            ring.append(lax.ppermute(value, AXES, pairs_))
        return jnp.stack(ring)

    whole = lambda *dims: pl.BlockSpec(dims, lambda k: (0,) * len(dims))
    scratch = [
        pltpu.VMEM((2, cells + slab, CHANNELS), jnp.float32),
        pltpu.VMEM((cells + slab, 4 * CHANNELS), jnp.bfloat16),
    ]

    def chain(forward, first, terms, kernel_pairs, slopes=None):
        order = (lambda k: k) if forward else (lambda k: members - 1 - k)
        term_spec = pl.BlockSpec(
            (1, zs) + terms.shape[2:], lambda k: (order(k), 0, 0, 0)
        )
        slope_spec = pl.BlockSpec(
            (1, 2, cells, CHANNELS), lambda k: (jnp.minimum(order(k), members - 2), 0, 0, 0)
        )
        received = None
        for turn in range(groups):
            opening, closing = turn == 0, turn == groups - 1
            operands = [meta if forward else back_meta, first]
            specs = [SMEM, whole(*first.shape)]
            if not opening:
                operands.append(received)
                specs.append(whole(*received.shape))
            if forward:
                operands += [terms, kernel_pairs, bias]
                specs += [term_spec, whole(*kernel_pairs.shape), whole(1, CHANNELS)]
            else:
                operands += [slopes, terms, kernel_pairs]
                specs += [slope_spec, term_spec, whole(*kernel_pairs.shape)]
            shapes, places = [shape_of(2, slab, CHANNELS)], [whole(2, slab, CHANNELS)]
            if closing:
                shapes += [shape_of(2, 2 * slab, CHANNELS), shape_of(2, slab, CHANNELS)]
                places += [whole(2, 2 * slab, CHANNELS), whole(2, slab, CHANNELS)]
                if forward:
                    shapes.append(shape_of(members - 1, 2, cells, CHANNELS))
                    places.append(slope_spec)
            leaving, *found = pl.pallas_call(
                functools.partial(chain_kernel, forward, opening, closing, zs),
                grid=(members,),
                out_shape=shapes,
                in_specs=specs,
                out_specs=places,
                scratch_shapes=scratch,
                compiler_params=pltpu.CompilerParams(
                    vmem_limit_bytes=60 * 1024 * 1024,
                    allow_input_fusion=[operand is terms for operand in operands],
                ),
                name="forward_chain" if forward else "backward_chain",
            )(*operands)
            if not closing:
                received = passed(leaving, 1 if forward else -1)
        return found

    terms = over_members(sent)
    starts = jnp.swapaxes(terms[:, :, 2 * slab :], 0, 1).astype(jnp.float32)
    starts = starts.reshape(zs, 2, slab, CHANNELS)
    terms = terms.astype(jnp.float32)
    before_slab, own_slab, slopes = chain(True, starts, terms, weights)

    guess_spec = pl.BlockSpec((None, row_count, cols, CHANNELS), lambda k: (1, 0, 0, 0))
    target_spec = pl.BlockSpec((None, row_count, cols, CHANNELS), lambda k: (0, 0, 0, 0))
    piece = [whole(2, cols, CHANNELS), whole(row_count, cols, CHANNELS), whole(2, cols, CHANNELS)]
    pair_spec = whole(12 * CHANNELS, 2 * CHANNELS)
    states, residual, even_taps, odd_taps, odd_slope = pl.pallas_call(
        functools.partial(correct_kernel, zs),
        grid=(1,),
        out_shape=(
            shape_of(2, row_count, cols, CHANNELS),
            shape_of(2 * slab, CHANNELS),
            shape_of(6 * pairs, 4 * CHANNELS, dtype=jnp.bfloat16),
            shape_of(6 * pairs, 4 * CHANNELS, dtype=jnp.bfloat16),
            shape_of(2, 4 * pairs, CHANNELS),
        ),
        in_specs=[SMEM]
        + piece
        + [guess_spec]
        + piece
        + [target_spec, whole(2, 2 * slab, CHANNELS), whole(2, slab, CHANNELS)]
        + [pair_spec, pair_spec, whole(1, CHANNELS)],
        out_specs=(
            whole(2, row_count, cols, CHANNELS),
            whole(2 * slab, CHANNELS),
            whole(6 * pairs, 4 * CHANNELS),
            whole(6 * pairs, 4 * CHANNELS),
            whole(2, 4 * pairs, CHANNELS),
        ),
        scratch_shapes=[
            pltpu.VMEM((8 * pairs, 4 * CHANNELS), jnp.bfloat16),
            pltpu.VMEM((4, pairs, CHANNELS), jnp.float32),
            pltpu.VMEM((pairs, CHANNELS), jnp.float32),
        ],
        compiler_params=PARAMS,
        name="correct",
    )(
        meta, *before, forward_guess, *ahead, adjoint_guess, before_slab, own_slab,
        weights, flipped, bias,
    )

    ahead_slab, error_slab = chain(
        False, starts, over_members(residual).astype(jnp.float32), flipped, slopes
    )

    scale = STEP_SIZE / (row_count * zs * cols)
    grad_rows = 9 * CHANNELS + CHANNELS
    adjoints, grads = pl.pallas_call(
        functools.partial(finish_kernel, scale),
        grid=(1,),
        out_shape=(shape_of(2, row_count, cols, CHANNELS), shape_of(grad_rows, CHANNELS)),
        in_specs=piece
        + [target_spec, whole(2, 2 * slab, CHANNELS), whole(2, slab, CHANNELS)]
        + [whole(6 * pairs, 4 * CHANNELS)] * 2
        + [whole(2, 4 * pairs, CHANNELS), pair_spec],
        out_specs=(whole(2, row_count, cols, CHANNELS), whole(grad_rows, CHANNELS)),
        scratch_shapes=[
            pltpu.VMEM((6 * pairs, 4 * CHANNELS), jnp.bfloat16),
            pltpu.VMEM((4, pairs, CHANNELS), jnp.float32),
        ],
        compiler_params=PARAMS,
        name="finish",
    )(
        *ahead, adjoint_guess, ahead_slab, error_slab, even_taps, odd_taps, odd_slope, flipped
    )

    share = grads.reshape(depth, grad_rows // depth, CHANNELS)
    deep = ("group", "member")
    share = lax.all_to_all(share, deep, 0, 0, tiled=True).sum(0)
    parts = [share] + [
        lax.ppermute(share, "rows", [(z, z ^ turn) for z in range(zs)]) for turn in range(1, zs)
    ]
    while len(parts) > 1:
        parts = [a + b for a, b in zip(parts[::2], parts[1::2])]
    share = parts[0]
    share = jnp.broadcast_to(share[None], (depth,) + share.shape)
    grads = lax.all_to_all(share, deep, 0, 0, tiled=True).reshape(grad_rows, CHANNELS)
    grad_kernel = grads[: 9 * CHANNELS].reshape(3, 3, CHANNELS, CHANNELS)
    return states, adjoints, grad_kernel, grads[9 * CHANNELS]


def solution(mesh):
    depth, rows = mesh.devices.shape
    own = Mesh(mesh.devices.reshape(GROUPS, depth // GROUPS, rows), AXES)
    deep = ("group", "member")
    placed = (
        P("rows", None, None),
        P(deep, "rows", None, None),
        P(deep, "rows", None, None),
        P("rows", None, None),
        P(),
        P(),
    )
    return jax.shard_map(
        shards,
        mesh=own,
        in_specs=placed,
        out_specs=(P(deep, "rows", None, None), P(deep, "rows", None, None), P(), P()),
        check_vma=False,
    )
```

```python
import functools

import jax
import jax.numpy as jnp
from jax import lax
from jax.experimental import pallas as pl
from jax.experimental.pallas import tpu as pltpu
from jax.sharding import Mesh, PartitionSpec as P

STEP_SIZE = 0.2
COARSE_SIZE = 2.0 * STEP_SIZE
CHUNK_SLABS = 4
AXES = ("depth", "rows")
CHANNELS = 128
SMEM = pl.BlockSpec(memory_space=pltpu.SMEM)
VMEM = pl.BlockSpec(memory_space=pltpu.VMEM)
PARAMS = pltpu.CompilerParams(vmem_limit_bytes=20 * 1024 * 1024)


def shape_of(*dims, dtype=jnp.float32):
    return jax.ShapeDtypeStruct(dims, dtype)


def spread(even, odd, width):
    count = even.shape[0]
    place = lax.broadcasted_iota(jnp.int32, even.shape, 0) % width
    before = jnp.where(place == 0, 0.0, pltpu.roll(odd, 1, 0))
    after = jnp.where(place == width - 1, 0.0, pltpu.roll(even, count - 1, 0))
    return jnp.concatenate([even, odd, before, after], axis=1).astype(jnp.bfloat16)


def taps(ref, start, count, width, weights):
    lhs = jnp.concatenate(
        [ref[start + tap * width : start + tap * width + count] for tap in range(3)], axis=1
    )
    return jnp.dot(lhs, weights, preferred_element_type=jnp.float32)


def halves(value):
    return value[:, :CHANNELS], value[:, CHANNELS:]


def pair_weights(kernel):
    none = jnp.zeros_like(kernel[:, 0])
    left, mid, right = kernel[:, 0], kernel[:, 1], kernel[:, 2]
    to_even = jnp.concatenate([mid, right, left, none], axis=1)
    to_odd = jnp.concatenate([left, mid, none, right], axis=1)
    return jnp.concatenate([to_even, to_odd], axis=2).reshape(12 * CHANNELS, 2 * CHANNELS)


def row_planes(ref, row, cols):
    return ref[row, pl.ds(0, cols // 2, stride=2), :], ref[row, pl.ds(1, cols // 2, stride=2), :]


def planes_of(refs_rows, cols):
    pairs = [row_planes(ref, row, cols) for ref, row in refs_rows]
    return jnp.concatenate([e for e, _ in pairs], 0), jnp.concatenate([o for _, o in pairs], 0)


def with_halo(top, main, bottom, halo):
    rows = [(top, 2 - halo + i) for i in range(halo)]
    rows += [(main, i) for i in range(main.shape[0])]
    return rows + [(bottom, i) for i in range(halo)]


def restricted(even, odd, pairs):
    both = even + odd
    return [
        (both[i * pairs : (i + 1) * pairs] + both[(i + 1) * pairs : (i + 2) * pairs]) * 0.25
        for i in range(0, both.shape[0] // pairs, 2)
    ]


def masked(value, pairs, at_top, at_bottom):
    count = value.shape[0] // pairs
    parts = [value[i * pairs : (i + 1) * pairs] for i in range(count)]
    parts[0] = jnp.where(at_top, jnp.zeros_like(parts[0]), parts[0])
    parts[-1] = jnp.where(at_bottom, jnp.zeros_like(parts[-1]), parts[-1])
    return jnp.concatenate(parts, 0)


def store_planes(out, scratch, rows, pairs):
    half = pairs // 2
    for i, row in enumerate(rows):
        scratch[...] = row
        for plane in range(2):
            base = (plane * len(rows) + i) * half
            out[base : base + half] = scratch[pl.ds(plane, half, stride=2), :]


def natural_rows(ref, scratch, count, pairs):
    half = pairs // 2
    rows = []
    for i in range(count):
        for plane in range(2):
            scratch[i, pl.ds(plane, half, stride=2), :] = ref[plane, i * half : (i + 1) * half]
        rows.append(scratch[i])
    return rows


def relax_kernel(
    shards_z, meta, top, main, bottom, first, weights, plain, bias, sent, fine, coarse, row, start
):
    pairs = main.shape[1] // 2
    at_top, at_bottom = meta[0] == 0, meta[0] == shards_z - 1
    even, odd = planes_of(with_halo(top, main, bottom, 2), main.shape[1])
    fine[...] = spread(jnp.tanh(even), jnp.tanh(odd), pairs)
    six = slice(pairs, 7 * pairs)
    conv_even, conv_odd = halves(taps(fine, 0, 6 * pairs, pairs, weights[...]))
    odd_even = masked(even[six] + STEP_SIZE * (conv_even + bias[...]), pairs, at_top, at_bottom)
    odd_odd = masked(odd[six] + STEP_SIZE * (conv_odd + bias[...]), pairs, at_top, at_bottom)
    fine[0 : 6 * pairs] = spread(jnp.tanh(odd_even), jnp.tanh(odd_odd), pairs)
    conv_even, conv_odd = halves(taps(fine, 0, 4 * pairs, pairs, weights[...]))
    four = slice(pairs, 5 * pairs)
    two_even = odd_even[four] + STEP_SIZE * (conv_even + bias[...])
    two_odd = odd_odd[four] + STEP_SIZE * (conv_odd + bias[...])
    fine_rows = restricted(two_even, two_odd, pairs)
    own = restricted(even, odd, pairs)
    place = lax.broadcasted_iota(jnp.int32, own[0].shape, 0)
    for i, value in enumerate(own):
        squashed = jnp.tanh(value)
        before = jnp.where(place == 0, 0.0, pltpu.roll(squashed, 1, 0))
        after = jnp.where(place == pairs - 1, 0.0, pltpu.roll(squashed, pairs - 1, 0))
        coarse[i * pairs : (i + 1) * pairs] = jnp.concatenate([before, squashed, after], 1).astype(
            jnp.bfloat16
        )
    conv = taps(coarse, 0, 2 * pairs, pairs, plain[...])
    rows = [
        fine_rows[i]
        - (own[i + 1] + COARSE_SIZE * (conv[i * pairs : (i + 1) * pairs] + bias[...]))
        for i in range(2)
    ]
    store_planes(sent, row, rows, pairs)
    even, odd = planes_of([(first, i) for i in range(4)], first.shape[1])
    store_planes(start, row, restricted(even, odd, pairs), pairs)
    share = sent.shape[0] - start.shape[0]
    sent[start.shape[0] :] = start[pl.ds(pl.multiple_of(meta[1] * share, share), share)]


def chain_kernel(forward, shards_z, chunk_slabs, meta, *refs):
    if forward:
        initial, terms, weights, bias, around_out, own_out, *slopes, state, taps_in = refs
    else:
        *slopes, terms, weights, around_out, own_out, state, taps_in = refs
    step, turns = pl.program_id(0), pl.num_programs(0)
    pos = meta[0]
    slab = own_out.shape[1]
    half = slab // 2
    cells = shards_z * slab

    @pl.when(step == 0)
    def _():
        state[...] = jnp.zeros_like(state)
        taps_in[...] = jnp.zeros_like(taps_in)
        if forward:
            for turn in range(shards_z):
                state[:, half + turn * slab : half + (turn + 1) * slab] = initial[turn]

    mine = meta[1] if forward else turns - 1 - meta[1]

    @pl.when(step == mine)
    def _():
        around_out[...] = state[:, pl.ds(pl.multiple_of(pos * slab, half), 2 * slab)]

    chunk = chunk_slabs * slab
    for start in range(0, cells, chunk):
        span = slice(half + start, half + start + chunk)
        even, odd = state[0, span], state[1, span]
        if forward:
            even, odd = jnp.tanh(even), jnp.tanh(odd)
            slopes[0][0, start : start + chunk] = COARSE_SIZE * (1.0 - even * even)
            slopes[1][0, start : start + chunk] = COARSE_SIZE * (1.0 - odd * odd)
        taps_in[span] = spread(even, odd, half)
    for start in range(0, cells, chunk):
        conv = halves(taps(taps_in, start, chunk, half, weights[...]))
        for plane in range(2):
            for j in range(chunk_slabs):
                low = start + j * slab
                part = conv[plane][j * slab : (j + 1) * slab]
                if forward:
                    moved = COARSE_SIZE * (part + bias[...])
                else:
                    moved = slopes[plane][0, low : low + slab] * part
                span = slice(half + low, half + low + slab)
                term = terms[0, low // slab, plane * slab : (plane + 1) * slab]
                state[plane, span] = state[plane, span] + moved + term

    @pl.when(step == mine)
    def _():
        own_out[...] = state[:, pl.ds(pl.multiple_of(half + pos * slab, half), slab)]


def correct_kernel(
    shards_z,
    meta,
    top,
    main,
    bottom,
    guess,
    ahead_top,
    ahead_main,
    ahead_bottom,
    target,
    before_slab,
    own_slab,
    weights,
    flipped,
    bias,
    states,
    residual,
    even_taps,
    odd_taps,
    odd_slope,
    fine,
    natural,
    row,
):
    cols = main.shape[1]
    pairs = cols // 2
    at_top, at_bottom = meta[0] == 0, meta[0] == shards_z - 1
    even, odd = planes_of(with_halo(top, main, bottom, 2), cols)
    rest = restricted(even, odd, pairs)
    found = natural_rows(before_slab, natural, 4, pairs)
    change = [jnp.where(meta[2] == 1, 0.0, a - b) for a, b in zip(found, rest)]
    change = jnp.concatenate([c for c in change for _ in range(2)], 0)
    even, odd = even + change, odd + change

    here, there = planes_of([(guess, i) for i in range(4)], cols)
    rest = restricted(here, there, pairs)
    found = natural_rows(own_slab, natural, 2, pairs)
    change = jnp.concatenate([a - b for a, b in zip(found, rest) for _ in range(2)], 0)
    here, there = here + change, there + change
    for i in range(4):
        span = slice(i * pairs, (i + 1) * pairs)
        states[1, i, pl.ds(0, pairs, stride=2), :] = here[span]
        states[1, i, pl.ds(1, pairs, stride=2), :] = there[span]

    tanh_even, tanh_odd = jnp.tanh(even), jnp.tanh(odd)
    fine[...] = spread(tanh_even, tanh_odd, pairs)
    six, four = slice(pairs, 7 * pairs), slice(pairs, 5 * pairs)
    even_taps[...] = fine[six]
    own = slice(2 * pairs, 6 * pairs)
    slope_even = STEP_SIZE * (1.0 - tanh_even[own] ** 2)
    slope_odd = STEP_SIZE * (1.0 - tanh_odd[own] ** 2)
    conv_even, conv_odd = halves(taps(fine, 0, 6 * pairs, pairs, weights[...]))
    even = masked(even[six] + STEP_SIZE * (conv_even + bias[...]), pairs, at_top, at_bottom)
    odd = masked(odd[six] + STEP_SIZE * (conv_odd + bias[...]), pairs, at_top, at_bottom)
    for i in range(4):
        span = slice((i + 1) * pairs, (i + 2) * pairs)
        states[0, i, pl.ds(0, pairs, stride=2), :] = even[span]
        states[0, i, pl.ds(1, pairs, stride=2), :] = odd[span]
    tanh_even, tanh_odd = jnp.tanh(even), jnp.tanh(odd)
    odd_taps[...] = spread(tanh_even, tanh_odd, pairs)
    step_even, step_odd = STEP_SIZE * (1.0 - tanh_even**2), STEP_SIZE * (1.0 - tanh_odd**2)
    odd_slope[0] = step_even[four]
    odd_slope[1] = step_odd[four]

    even, odd = planes_of(with_halo(ahead_top, ahead_main, ahead_bottom, 2), cols)
    fine[...] = spread(even, odd, pairs)
    conv_even, conv_odd = halves(taps(fine, 0, 6 * pairs, pairs, flipped[...]))
    even = masked(even[six] + step_even * conv_even, pairs, at_top, at_bottom)
    odd = masked(odd[six] + step_odd * conv_odd, pairs, at_top, at_bottom)
    fine[0 : 6 * pairs] = spread(even, odd, pairs)
    conv_even, conv_odd = halves(taps(fine, 0, 4 * pairs, pairs, flipped[...]))
    here, there = planes_of([(target, i) for i in range(4)], cols)
    even = even[four] + slope_even * conv_even - here
    odd = odd[four] + slope_odd * conv_odd - there
    store_planes(residual, row, restricted(even, odd, pairs), pairs)


def finish_kernel(
    scale,
    top,
    main,
    bottom,
    target,
    ahead_slab,
    own_slab,
    even_taps,
    odd_taps,
    odd_slope,
    flipped,
    adjoints,
    grads,
    fine,
    natural,
):
    cols = main.shape[1]
    pairs = cols // 2
    here, there = planes_of([(target, i) for i in range(4)], cols)
    change = natural_rows(own_slab, natural, 2, pairs)
    change = jnp.concatenate([c for c in change for _ in range(2)], 0)
    here, there = here + change, there + change
    for i in range(4):
        span = slice(i * pairs, (i + 1) * pairs)
        adjoints[0, i, pl.ds(0, pairs, stride=2), :] = here[span]
        adjoints[0, i, pl.ds(1, pairs, stride=2), :] = there[span]
    even, odd = planes_of(with_halo(top, main, bottom, 1), cols)
    found = natural_rows(ahead_slab, natural, 4, pairs)
    change = jnp.concatenate([found[0], found[1], found[1], found[2], found[2], found[3]], 0)
    even, odd = even + change, odd + change
    fine[...] = spread(even, odd, pairs)
    conv_even, conv_odd = halves(taps(fine, 0, 4 * pairs, pairs, flipped[...]))
    four = slice(pairs, 5 * pairs)
    even, odd = even[four], odd[four]
    new_even, new_odd = even + odd_slope[0] * conv_even, odd + odd_slope[1] * conv_odd
    for i in range(4):
        span = slice(i * pairs, (i + 1) * pairs)
        adjoints[1, i, pl.ds(0, pairs, stride=2), :] = new_even[span]
        adjoints[1, i, pl.ds(1, pairs, stride=2), :] = new_odd[span]
    right = jnp.concatenate(
        [
            jnp.concatenate([new_even, new_odd], 1).astype(jnp.bfloat16),
            jnp.concatenate([even, odd], 1).astype(jnp.bfloat16),
        ],
        0,
    )
    one, two, three, four_ = (slice(i * CHANNELS, (i + 1) * CHANNELS) for i in range(4))
    for tap in range(3):
        span = slice(tap * pairs, (tap + 4) * pairs)
        left = jnp.concatenate([even_taps[span], odd_taps[span]], 0)
        found = lax.dot_general(
            left, right, (((0,), (0,)), ((), ())), preferred_element_type=jnp.float32
        )
        base = tap * 3 * CHANNELS
        grads[base : base + CHANNELS] = scale * (found[one, two] + found[three, one])
        grads[base + CHANNELS : base + 2 * CHANNELS] = scale * (found[one, one] + found[two, two])
        grads[base + 2 * CHANNELS : base + 3 * CHANNELS] = scale * (
            found[two, one] + found[four_, two]
        )
    total = jnp.sum(new_even + new_odd + even + odd, axis=0, keepdims=True)
    base = 9 * CHANNELS
    rest = grads.shape[0] - base
    place = lax.broadcasted_iota(jnp.int32, (rest, CHANNELS), 0)
    grads[base:] = jnp.where(place == 0, scale * total, 0.0)


def shards(initial, forward_guess, adjoint_guess, cotangent, kernel, conv_bias):
    depth, zs = (lax.axis_size(axis) for axis in AXES)
    index, pos = (lax.axis_index(axis) for axis in AXES)
    at_first, at_last = index == 0, index == depth - 1
    row_count, cols, _ = initial.shape
    pairs = cols // 2
    slab = 2 * pairs // 2
    cells = zs * slab
    bias = conv_bias.reshape(1, CHANNELS)
    meta = jnp.stack([pos, index, at_first]).astype(jnp.int32)

    def moved(value, along, across):
        pairs_ = [
            (d * zs + z, (d + along) % depth * zs + z + across)
            for d in range(depth)
            for z in range(zs)
            if 0 <= z + across < zs
        ]
        return lax.ppermute(value, AXES, pairs_)

    main = jnp.where(at_last, initial, forward_guess[1])
    held = (moved(main[row_count - 2 :], 0, 1), main, moved(main[:2], 0, -1))
    target_sent = jnp.where(at_first, cotangent, adjoint_guess[0])

    weights = pair_weights(kernel)
    plain = kernel.reshape(9 * CHANNELS, CHANNELS)
    flipped = pair_weights(jnp.transpose(jnp.flip(kernel, (0, 1)), (0, 1, 3, 2)))

    share = 2 * slab // depth
    sent = pl.pallas_call(
        functools.partial(relax_kernel, zs),
        out_shape=shape_of(2 * slab + share, CHANNELS),
        in_specs=[SMEM] + [VMEM] * 7,
        out_specs=VMEM,
        scratch_shapes=[
            pltpu.VMEM((8 * pairs, 4 * CHANNELS), jnp.bfloat16),
            pltpu.VMEM((4 * pairs, 3 * CHANNELS), jnp.bfloat16),
            pltpu.VMEM((pairs, CHANNELS), jnp.float32),
            pltpu.VMEM((2 * slab, CHANNELS), jnp.float32),
        ],
        compiler_params=PARAMS,
        name="relax",
    )(meta, *held, initial, weights, plain, bias)

    def over_rows(value):
        gathered = jnp.zeros((zs,) + value.shape, value.dtype)
        for turn in range(zs):
            place = lax.rem(pos + turn, zs)
            if turn:
                ring = [((i + turn) % zs, i) for i in range(zs)]
                part = lax.ppermute(value, "rows", ring)
            else:
                part = value
            gathered = lax.dynamic_update_slice_in_dim(gathered, part[None], place, 0)
        return gathered

    def over_all(value):
        return lax.all_gather(over_rows(value.astype(jnp.float16)), "depth")

    whole = lambda *dims: pl.BlockSpec(dims, lambda k: (0,) * len(dims))

    def chain(forward, terms, kernel_pairs, extra):
        term_at = (lambda k: lax.rem(k + depth - 1, depth)) if forward else (lambda k: depth - 1 - k)
        slope_at = (lambda k: k) if forward else term_at
        term_spec = pl.BlockSpec((1, zs) + terms.shape[2:], lambda k: (term_at(k), 0, 0, 0))
        slope_spec = pl.BlockSpec((1, cells, CHANNELS), lambda k: (slope_at(k), 0, 0))
        shapes = [shape_of(2, 2 * slab, CHANNELS), shape_of(2, slab, CHANNELS)]
        places = [whole(2, 2 * slab, CHANNELS), whole(2, slab, CHANNELS)]
        pair_spec = whole(*kernel_pairs.shape)
        if forward:
            operands = [meta, extra, terms, kernel_pairs, bias]
            specs = [SMEM, whole(*extra.shape), term_spec, pair_spec, whole(1, CHANNELS)]
            shapes += [shape_of(depth, cells, CHANNELS)] * 2
            places += [slope_spec] * 2
        else:
            operands = [meta, *extra, terms, kernel_pairs]
            specs = [SMEM, slope_spec, slope_spec, term_spec, pair_spec]
        return pl.pallas_call(
            functools.partial(chain_kernel, forward, zs, CHUNK_SLABS),
            grid=(depth,),
            out_shape=shapes,
            in_specs=specs,
            out_specs=places,
            scratch_shapes=[
                pltpu.VMEM((2, cells + slab, CHANNELS), jnp.float32),
                pltpu.VMEM((cells + slab, 4 * CHANNELS), jnp.bfloat16),
            ],
            compiler_params=pltpu.CompilerParams(
                vmem_limit_bytes=24 * 1024 * 1024,
                allow_input_fusion=[operand is terms for operand in operands],
            ),
            name="forward_chain" if forward else "backward_chain",
        )(*operands)

    terms = over_all(sent)
    starts = jnp.swapaxes(terms[:, :, 2 * slab :], 0, 1).astype(jnp.float32)
    starts = starts.reshape(zs, 2, slab, CHANNELS)
    starts, held, target_sent = lax.optimization_barrier((starts, held, target_sent))
    before = tuple(moved(part, 1, 0) for part in held)
    ahead = (
        moved(target_sent[row_count - 2 :], -1, 1),
        moved(target_sent, -1, 0),
        moved(target_sent[:2], -1, -1),
    )
    before_slab, own_slab, *slopes = chain(True, terms.astype(jnp.float32), weights, starts)

    states, residual, even_taps, odd_taps, odd_slope = pl.pallas_call(
        functools.partial(correct_kernel, zs),
        out_shape=(
            shape_of(2, row_count, cols, CHANNELS),
            shape_of(2 * slab, CHANNELS),
            shape_of(6 * pairs, 4 * CHANNELS, dtype=jnp.bfloat16),
            shape_of(6 * pairs, 4 * CHANNELS, dtype=jnp.bfloat16),
            shape_of(2, 4 * pairs, CHANNELS),
        ),
        in_specs=[SMEM] + [VMEM] * 13,
        out_specs=(VMEM,) * 5,
        scratch_shapes=[
            pltpu.VMEM((8 * pairs, 4 * CHANNELS), jnp.bfloat16),
            pltpu.VMEM((4, pairs, CHANNELS), jnp.float32),
            pltpu.VMEM((pairs, CHANNELS), jnp.float32),
        ],
        compiler_params=PARAMS,
        name="correct",
    )(
        meta, *before, forward_guess[1], *ahead, adjoint_guess[0], before_slab, own_slab,
        weights, flipped, bias,
    )

    terms = over_all(residual).astype(jnp.float32)
    ahead_slab, error_slab = chain(False, terms, flipped, slopes)

    scale = STEP_SIZE / (row_count * zs * cols)
    grad_rows = 9 * CHANNELS + CHANNELS
    adjoints, grads = pl.pallas_call(
        functools.partial(finish_kernel, scale),
        out_shape=(shape_of(2, row_count, cols, CHANNELS), shape_of(grad_rows, CHANNELS)),
        in_specs=[VMEM] * 10,
        out_specs=(VMEM, VMEM),
        scratch_shapes=[
            pltpu.VMEM((6 * pairs, 4 * CHANNELS), jnp.bfloat16),
            pltpu.VMEM((4, pairs, CHANNELS), jnp.float32),
        ],
        compiler_params=PARAMS,
        name="finish",
    )(
        *ahead, adjoint_guess[0], ahead_slab, error_slab, even_taps, odd_taps, odd_slope, flipped
    )

    share = grads.reshape(depth, grad_rows // depth, CHANNELS)
    share = lax.all_to_all(share, "depth", 0, 0, tiled=True).sum(0)
    parts = [share] + [
        lax.ppermute(share, "rows", [(z, z ^ turn) for z in range(zs)]) for turn in range(1, zs)
    ]
    while len(parts) > 1:
        parts = [a + b for a, b in zip(parts[::2], parts[1::2])]
    share = parts[0]
    share = jnp.broadcast_to(share[None], (depth,) + share.shape)
    grads = lax.all_to_all(share, "depth", 0, 0, tiled=True).reshape(grad_rows, CHANNELS)
    grad_kernel = grads[: 9 * CHANNELS].reshape(3, 3, CHANNELS, CHANNELS)
    return states, adjoints, grad_kernel, grads[9 * CHANNELS]


def solution(mesh):
    placed = (
        P("rows", None, None),
        P("depth", "rows", None, None),
        P("depth", "rows", None, None),
        P("rows", None, None),
        P(),
        P(),
    )
    return jax.shard_map(
        shards,
        mesh=mesh,
        in_specs=placed,
        out_specs=(P("depth", "rows", None, None), P("depth", "rows", None, None), P(), P()),
        check_vma=False,
    )
```

```python
import functools

import jax
import jax.numpy as jnp
from jax import lax
from jax.experimental import pallas as pl
from jax.experimental.pallas import tpu as pltpu
from jax.sharding import Mesh, PartitionSpec as P

STEP_SIZE = 0.2
COARSE_SIZE = 2.0 * STEP_SIZE
CHUNK_SLABS = 8
AXES = ("depth", "rows")
CHANNELS = 128
SMEM = pl.BlockSpec(memory_space=pltpu.SMEM)
VMEM = pl.BlockSpec(memory_space=pltpu.VMEM)
PARAMS = pltpu.CompilerParams(vmem_limit_bytes=20 * 1024 * 1024)


def shape_of(*dims, dtype=jnp.float32):
    return jax.ShapeDtypeStruct(dims, dtype)


def spread(even, odd, width):
    count = even.shape[0]
    place = lax.broadcasted_iota(jnp.int32, even.shape, 0) % width
    before = jnp.where(place == 0, 0.0, pltpu.roll(odd, 1, 0))
    after = jnp.where(place == width - 1, 0.0, pltpu.roll(even, count - 1, 0))
    return jnp.concatenate([even, odd, before, after], axis=1).astype(jnp.bfloat16)


def taps(ref, start, count, width, weights):
    lhs = jnp.concatenate(
        [ref[start + tap * width : start + tap * width + count] for tap in range(3)], axis=1
    )
    return jnp.dot(lhs, weights, preferred_element_type=jnp.float32)


def halves(value):
    return value[:, :CHANNELS], value[:, CHANNELS:]


def pair_weights(kernel):
    none = jnp.zeros_like(kernel[:, 0])
    left, mid, right = kernel[:, 0], kernel[:, 1], kernel[:, 2]
    to_even = jnp.concatenate([mid, right, left, none], axis=1)
    to_odd = jnp.concatenate([left, mid, none, right], axis=1)
    return jnp.concatenate([to_even, to_odd], axis=2).reshape(12 * CHANNELS, 2 * CHANNELS)


def pack_weights(packed, pairs):
    packed[6 * CHANNELS :] = jnp.zeros((8 * CHANNELS, 2 * CHANNELS), packed.dtype)
    for tap in range(3):
        base = 4 * tap * CHANNELS
        packed[2 * tap * CHANNELS : 2 * (tap + 1) * CHANNELS] = pairs[base : base + 2 * CHANNELS]
        for plane in range(2):
            row = base + (2 + plane) * CHANNELS
            side = pairs[row : row + CHANNELS, plane * CHANNELS : (plane + 1) * CHANNELS]
            low = (6 + 4 * plane + tap) * CHANNELS
            packed[low : low + CHANNELS, :CHANNELS] = side
            packed[low + CHANNELS : low + 2 * CHANNELS, CHANNELS:] = side


def row_planes(ref, row, cols):
    return ref[row, pl.ds(0, cols // 2, stride=2), :], ref[row, pl.ds(1, cols // 2, stride=2), :]


def planes_of(refs_rows, cols):
    pairs = [row_planes(ref, row, cols) for ref, row in refs_rows]
    return jnp.concatenate([e for e, _ in pairs], 0), jnp.concatenate([o for _, o in pairs], 0)


def with_halo(top, main, bottom, halo):
    rows = [(top, 2 - halo + i) for i in range(halo)]
    rows += [(main, i) for i in range(main.shape[0])]
    return rows + [(bottom, i) for i in range(halo)]


def restricted(even, odd, pairs):
    both = even + odd
    return [
        (both[i * pairs : (i + 1) * pairs] + both[(i + 1) * pairs : (i + 2) * pairs]) * 0.25
        for i in range(0, both.shape[0] // pairs, 2)
    ]


def masked(value, pairs, at_top, at_bottom):
    count = value.shape[0] // pairs
    parts = [value[i * pairs : (i + 1) * pairs] for i in range(count)]
    parts[0] = jnp.where(at_top, jnp.zeros_like(parts[0]), parts[0])
    parts[-1] = jnp.where(at_bottom, jnp.zeros_like(parts[-1]), parts[-1])
    return jnp.concatenate(parts, 0)


def store_planes(out, scratch, rows, pairs):
    half = pairs // 2
    for i, row in enumerate(rows):
        scratch[...] = row
        for plane in range(2):
            base = (plane * len(rows) + i) * half
            out[base : base + half] = scratch[pl.ds(plane, half, stride=2), :]


def natural_rows(ref, scratch, count, pairs):
    half = pairs // 2
    rows = []
    for i in range(count):
        for plane in range(2):
            scratch[i, pl.ds(plane, half, stride=2), :] = ref[plane, i * half : (i + 1) * half]
        rows.append(scratch[i])
    return rows


def relax_kernel(
    shards_z, meta, top, main, bottom, first, weights, plain, bias, sent, fine, coarse, row, start
):
    pairs = main.shape[1] // 2
    at_top, at_bottom = meta[0] == 0, meta[0] == shards_z - 1
    even, odd = planes_of(with_halo(top, main, bottom, 2), main.shape[1])
    fine[...] = spread(jnp.tanh(even), jnp.tanh(odd), pairs)
    six = slice(pairs, 7 * pairs)
    conv_even, conv_odd = halves(taps(fine, 0, 6 * pairs, pairs, weights[...]))
    odd_even = masked(even[six] + STEP_SIZE * (conv_even + bias[...]), pairs, at_top, at_bottom)
    odd_odd = masked(odd[six] + STEP_SIZE * (conv_odd + bias[...]), pairs, at_top, at_bottom)
    fine[0 : 6 * pairs] = spread(jnp.tanh(odd_even), jnp.tanh(odd_odd), pairs)
    conv_even, conv_odd = halves(taps(fine, 0, 4 * pairs, pairs, weights[...]))
    four = slice(pairs, 5 * pairs)
    two_even = odd_even[four] + STEP_SIZE * (conv_even + bias[...])
    two_odd = odd_odd[four] + STEP_SIZE * (conv_odd + bias[...])
    fine_rows = restricted(two_even, two_odd, pairs)
    own = restricted(even, odd, pairs)
    place = lax.broadcasted_iota(jnp.int32, own[0].shape, 0)
    for i, value in enumerate(own):
        squashed = jnp.tanh(value)
        before = jnp.where(place == 0, 0.0, pltpu.roll(squashed, 1, 0))
        after = jnp.where(place == pairs - 1, 0.0, pltpu.roll(squashed, pairs - 1, 0))
        coarse[i * pairs : (i + 1) * pairs] = jnp.concatenate([before, squashed, after], 1).astype(
            jnp.bfloat16
        )
    conv = taps(coarse, 0, 2 * pairs, pairs, plain[...])
    rows = [
        fine_rows[i]
        - (own[i + 1] + COARSE_SIZE * (conv[i * pairs : (i + 1) * pairs] + bias[...]))
        for i in range(2)
    ]
    store_planes(sent, row, rows, pairs)
    even, odd = planes_of([(first, i) for i in range(4)], first.shape[1])
    store_planes(start, row, restricted(even, odd, pairs), pairs)
    share = sent.shape[0] - start.shape[0]
    sent[start.shape[0] :] = start[pl.ds(pl.multiple_of(meta[1] * share, share), share)]


def chain_kernel(forward, shards_z, chunk_slabs, meta, *refs):
    if forward:
        initial, terms, pairs, bias, around_out, own_out, *slopes, state, taps_in, weights = refs
    else:
        *slopes, terms, pairs, around_out, own_out, state, taps_in, weights = refs
    step, turns = pl.program_id(0), pl.num_programs(0)
    pos = meta[0]
    slab = own_out.shape[1]
    half = slab // 2
    cells = shards_z * slab

    @pl.when(step == 0)
    def _():
        state[...] = jnp.zeros_like(state)
        taps_in[...] = jnp.zeros_like(taps_in)
        pack_weights(weights, pairs)
        if forward:
            for turn in range(shards_z):
                state[:, half + turn * slab : half + (turn + 1) * slab] = initial[turn]

    mine = meta[1] if forward else turns - 1 - meta[1]

    @pl.when(step == mine)
    def _():
        around_out[...] = state[:, pl.ds(pl.multiple_of(pos * slab, half), 2 * slab)]

    chunk = chunk_slabs * slab
    for start in range(0, cells, chunk):
        span = slice(half + start, half + start + chunk)
        even, odd = state[0, span], state[1, span]
        if forward:
            even, odd = jnp.tanh(even), jnp.tanh(odd)
            slopes[0][0, start : start + chunk] = COARSE_SIZE * (1.0 - even * even)
            slopes[1][0, start : start + chunk] = COARSE_SIZE * (1.0 - odd * odd)
        taps_in[span] = spread(even, odd, half)
    for start in range(0, cells, chunk):
        own = jnp.concatenate(
            [taps_in[start + t * half : start + t * half + chunk, : 2 * CHANNELS] for t in range(3)],
            axis=1,
        )
        own = halves(
            jnp.dot(own, weights[: 6 * CHANNELS], preferred_element_type=jnp.float32)
        )
        sides = []
        for plane in range(2):
            lanes = slice((2 + plane) * CHANNELS, (3 + plane) * CHANNELS)
            columns = []
            for t in range(4):
                first = start + t * half
                columns.append(
                    jnp.concatenate(
                        [
                            taps_in[first + j * slab : first + j * slab + half, lanes]
                            for j in range(chunk_slabs)
                        ],
                        axis=0,
                    )
                )
            base = (6 + 4 * plane) * CHANNELS
            sides.append(
                jnp.dot(
                    jnp.concatenate(columns, axis=1),
                    weights[base : base + 4 * CHANNELS],
                    preferred_element_type=jnp.float32,
                )
            )
        for plane in range(2):
            for j in range(2 * chunk_slabs):
                low = start + j * half
                side = sides[plane][j // 2 * half : (j // 2 + 1) * half]
                part = own[plane][j * half : (j + 1) * half] + halves(side)[j % 2]
                if forward:
                    moved = COARSE_SIZE * (part + bias[...])
                else:
                    moved = slopes[plane][0, low : low + half] * part
                span = slice(half + low, half + low + half)
                first = plane * slab + j % 2 * half
                term = terms[0, low // slab, first : first + half]
                state[plane, span] = state[plane, span] + moved + term

    @pl.when(step == mine)
    def _():
        own_out[...] = state[:, pl.ds(pl.multiple_of(half + pos * slab, half), slab)]


def correct_kernel(
    shards_z,
    meta,
    top,
    main,
    bottom,
    guess,
    ahead_top,
    ahead_main,
    ahead_bottom,
    target,
    before_slab,
    own_slab,
    weights,
    flipped,
    bias,
    states,
    residual,
    even_taps,
    odd_taps,
    odd_slope,
    fine,
    natural,
    row,
):
    cols = main.shape[1]
    pairs = cols // 2
    at_top, at_bottom = meta[0] == 0, meta[0] == shards_z - 1
    even, odd = planes_of(with_halo(top, main, bottom, 2), cols)
    rest = restricted(even, odd, pairs)
    found = natural_rows(before_slab, natural, 4, pairs)
    change = [jnp.where(meta[2] == 1, 0.0, a - b) for a, b in zip(found, rest)]
    change = jnp.concatenate([c for c in change for _ in range(2)], 0)
    even, odd = even + change, odd + change

    here, there = planes_of([(guess, i) for i in range(4)], cols)
    rest = restricted(here, there, pairs)
    found = natural_rows(own_slab, natural, 2, pairs)
    change = jnp.concatenate([a - b for a, b in zip(found, rest) for _ in range(2)], 0)
    here, there = here + change, there + change
    for i in range(4):
        span = slice(i * pairs, (i + 1) * pairs)
        states[1, i, pl.ds(0, pairs, stride=2), :] = here[span]
        states[1, i, pl.ds(1, pairs, stride=2), :] = there[span]

    tanh_even, tanh_odd = jnp.tanh(even), jnp.tanh(odd)
    fine[...] = spread(tanh_even, tanh_odd, pairs)
    six, four = slice(pairs, 7 * pairs), slice(pairs, 5 * pairs)
    even_taps[...] = fine[six]
    own = slice(2 * pairs, 6 * pairs)
    slope_even = STEP_SIZE * (1.0 - tanh_even[own] ** 2)
    slope_odd = STEP_SIZE * (1.0 - tanh_odd[own] ** 2)
    conv_even, conv_odd = halves(taps(fine, 0, 6 * pairs, pairs, weights[...]))
    even = masked(even[six] + STEP_SIZE * (conv_even + bias[...]), pairs, at_top, at_bottom)
    odd = masked(odd[six] + STEP_SIZE * (conv_odd + bias[...]), pairs, at_top, at_bottom)
    for i in range(4):
        span = slice((i + 1) * pairs, (i + 2) * pairs)
        states[0, i, pl.ds(0, pairs, stride=2), :] = even[span]
        states[0, i, pl.ds(1, pairs, stride=2), :] = odd[span]
    tanh_even, tanh_odd = jnp.tanh(even), jnp.tanh(odd)
    odd_taps[...] = spread(tanh_even, tanh_odd, pairs)
    step_even, step_odd = STEP_SIZE * (1.0 - tanh_even**2), STEP_SIZE * (1.0 - tanh_odd**2)
    odd_slope[0] = step_even[four]
    odd_slope[1] = step_odd[four]

    even, odd = planes_of(with_halo(ahead_top, ahead_main, ahead_bottom, 2), cols)
    fine[...] = spread(even, odd, pairs)
    conv_even, conv_odd = halves(taps(fine, 0, 6 * pairs, pairs, flipped[...]))
    even = masked(even[six] + step_even * conv_even, pairs, at_top, at_bottom)
    odd = masked(odd[six] + step_odd * conv_odd, pairs, at_top, at_bottom)
    fine[0 : 6 * pairs] = spread(even, odd, pairs)
    conv_even, conv_odd = halves(taps(fine, 0, 4 * pairs, pairs, flipped[...]))
    here, there = planes_of([(target, i) for i in range(4)], cols)
    even = even[four] + slope_even * conv_even - here
    odd = odd[four] + slope_odd * conv_odd - there
    store_planes(residual, row, restricted(even, odd, pairs), pairs)


def finish_kernel(
    scale,
    top,
    main,
    bottom,
    target,
    ahead_slab,
    own_slab,
    even_taps,
    odd_taps,
    odd_slope,
    flipped,
    adjoints,
    grads,
    fine,
    natural,
):
    cols = main.shape[1]
    pairs = cols // 2
    here, there = planes_of([(target, i) for i in range(4)], cols)
    change = natural_rows(own_slab, natural, 2, pairs)
    change = jnp.concatenate([c for c in change for _ in range(2)], 0)
    here, there = here + change, there + change
    for i in range(4):
        span = slice(i * pairs, (i + 1) * pairs)
        adjoints[0, i, pl.ds(0, pairs, stride=2), :] = here[span]
        adjoints[0, i, pl.ds(1, pairs, stride=2), :] = there[span]
    even, odd = planes_of(with_halo(top, main, bottom, 1), cols)
    found = natural_rows(ahead_slab, natural, 4, pairs)
    change = jnp.concatenate([found[0], found[1], found[1], found[2], found[2], found[3]], 0)
    even, odd = even + change, odd + change
    fine[...] = spread(even, odd, pairs)
    conv_even, conv_odd = halves(taps(fine, 0, 4 * pairs, pairs, flipped[...]))
    four = slice(pairs, 5 * pairs)
    even, odd = even[four], odd[four]
    new_even, new_odd = even + odd_slope[0] * conv_even, odd + odd_slope[1] * conv_odd
    for i in range(4):
        span = slice(i * pairs, (i + 1) * pairs)
        adjoints[1, i, pl.ds(0, pairs, stride=2), :] = new_even[span]
        adjoints[1, i, pl.ds(1, pairs, stride=2), :] = new_odd[span]
    right = jnp.concatenate(
        [
            jnp.concatenate([new_even, new_odd], 1).astype(jnp.bfloat16),
            jnp.concatenate([even, odd], 1).astype(jnp.bfloat16),
        ],
        0,
    )
    one, two, three, four_ = (slice(i * CHANNELS, (i + 1) * CHANNELS) for i in range(4))
    for tap in range(3):
        span = slice(tap * pairs, (tap + 4) * pairs)
        left = jnp.concatenate([even_taps[span], odd_taps[span]], 0)
        found = lax.dot_general(
            left, right, (((0,), (0,)), ((), ())), preferred_element_type=jnp.float32
        )
        base = tap * 3 * CHANNELS
        grads[base : base + CHANNELS] = scale * (found[one, two] + found[three, one])
        grads[base + CHANNELS : base + 2 * CHANNELS] = scale * (found[one, one] + found[two, two])
        grads[base + 2 * CHANNELS : base + 3 * CHANNELS] = scale * (
            found[two, one] + found[four_, two]
        )
    total = jnp.sum(new_even + new_odd + even + odd, axis=0, keepdims=True)
    base = 9 * CHANNELS
    rest = grads.shape[0] - base
    place = lax.broadcasted_iota(jnp.int32, (rest, CHANNELS), 0)
    grads[base:] = jnp.where(place == 0, scale * total, 0.0)


def shards(initial, forward_guess, adjoint_guess, cotangent, kernel, conv_bias):
    depth, zs = (lax.axis_size(axis) for axis in AXES)
    index, pos = (lax.axis_index(axis) for axis in AXES)
    at_first, at_last = index == 0, index == depth - 1
    row_count, cols, _ = initial.shape
    pairs = cols // 2
    slab = 2 * pairs // 2
    cells = zs * slab
    bias = conv_bias.reshape(1, CHANNELS)
    meta = jnp.stack([pos, index, at_first]).astype(jnp.int32)

    def moved(value, along, across):
        pairs_ = [
            (d * zs + z, (d + along) % depth * zs + z + across)
            for d in range(depth)
            for z in range(zs)
            if 0 <= z + across < zs
        ]
        return lax.ppermute(value, AXES, pairs_)

    main = jnp.where(at_last, initial, forward_guess[1])
    held = (moved(main[row_count - 2 :], 0, 1), main, moved(main[:2], 0, -1))
    target_sent = jnp.where(at_first, cotangent, adjoint_guess[0])

    weights = pair_weights(kernel)
    plain = kernel.reshape(9 * CHANNELS, CHANNELS)
    back_kernel = jnp.transpose(jnp.flip(kernel, (0, 1)), (0, 1, 3, 2))
    flipped = pair_weights(back_kernel)

    share = 2 * slab // depth
    sent = pl.pallas_call(
        functools.partial(relax_kernel, zs),
        out_shape=shape_of(2 * slab + share, CHANNELS),
        in_specs=[SMEM] + [VMEM] * 7,
        out_specs=VMEM,
        scratch_shapes=[
            pltpu.VMEM((8 * pairs, 4 * CHANNELS), jnp.bfloat16),
            pltpu.VMEM((4 * pairs, 3 * CHANNELS), jnp.bfloat16),
            pltpu.VMEM((pairs, CHANNELS), jnp.float32),
            pltpu.VMEM((2 * slab, CHANNELS), jnp.float32),
        ],
        compiler_params=PARAMS,
        name="relax",
    )(meta, *held, initial, weights, plain, bias)

    def over_rows(value):
        gathered = jnp.zeros((zs,) + value.shape, value.dtype)
        for turn in range(zs):
            place = lax.rem(pos + turn, zs)
            if turn:
                ring = [((i + turn) % zs, i) for i in range(zs)]
                part = lax.ppermute(value, "rows", ring)
            else:
                part = value
            gathered = lax.dynamic_update_slice_in_dim(gathered, part[None], place, 0)
        return gathered

    def over_all(value):
        return lax.all_gather(over_rows(value.astype(jnp.float16)), "depth")

    whole = lambda *dims: pl.BlockSpec(dims, lambda k: (0,) * len(dims))

    def chain(forward, terms, kernel_pairs, extra):
        term_at = (lambda k: lax.rem(k + depth - 1, depth)) if forward else (lambda k: depth - 1 - k)
        slope_at = (lambda k: k) if forward else term_at
        term_spec = pl.BlockSpec((1, zs) + terms.shape[2:], lambda k: (term_at(k), 0, 0, 0))
        slope_spec = pl.BlockSpec((1, cells, CHANNELS), lambda k: (slope_at(k), 0, 0))
        shapes = [shape_of(2, 2 * slab, CHANNELS), shape_of(2, slab, CHANNELS)]
        places = [whole(2, 2 * slab, CHANNELS), whole(2, slab, CHANNELS)]
        pair_spec = whole(*kernel_pairs.shape)
        if forward:
            operands = [meta, extra, terms, kernel_pairs, bias]
            specs = [SMEM, whole(*extra.shape), term_spec, pair_spec, whole(1, CHANNELS)]
            shapes += [shape_of(depth, cells, CHANNELS)] * 2
            places += [slope_spec] * 2
        else:
            operands = [meta, *extra, terms, kernel_pairs]
            specs = [SMEM, slope_spec, slope_spec, term_spec, pair_spec]
        return pl.pallas_call(
            functools.partial(chain_kernel, forward, zs, CHUNK_SLABS),
            grid=(depth,),
            out_shape=shapes,
            in_specs=specs,
            out_specs=places,
            scratch_shapes=[
                pltpu.VMEM((2, cells + slab, CHANNELS), jnp.float32),
                pltpu.VMEM((cells + slab, 4 * CHANNELS), jnp.bfloat16),
                pltpu.VMEM((14 * CHANNELS, 2 * CHANNELS), jnp.bfloat16),
            ],
            compiler_params=pltpu.CompilerParams(
                vmem_limit_bytes=24 * 1024 * 1024,
                allow_input_fusion=[operand is terms for operand in operands],
            ),
            name="forward_chain" if forward else "backward_chain",
        )(*operands)

    terms = over_all(sent)
    starts = jnp.swapaxes(terms[:, :, 2 * slab :], 0, 1).astype(jnp.float32)
    starts = starts.reshape(zs, 2, slab, CHANNELS)
    starts, held, target_sent = lax.optimization_barrier((starts, held, target_sent))
    before = tuple(moved(part, 1, 0) for part in held)
    ahead = (
        moved(target_sent[row_count - 2 :], -1, 1),
        moved(target_sent, -1, 0),
        moved(target_sent[:2], -1, -1),
    )
    before_slab, own_slab, *slopes = chain(
        True, terms.astype(jnp.float32), weights, starts
    )

    states, residual, even_taps, odd_taps, odd_slope = pl.pallas_call(
        functools.partial(correct_kernel, zs),
        out_shape=(
            shape_of(2, row_count, cols, CHANNELS),
            shape_of(2 * slab, CHANNELS),
            shape_of(6 * pairs, 4 * CHANNELS, dtype=jnp.bfloat16),
            shape_of(6 * pairs, 4 * CHANNELS, dtype=jnp.bfloat16),
            shape_of(2, 4 * pairs, CHANNELS),
        ),
        in_specs=[SMEM] + [VMEM] * 13,
        out_specs=(VMEM,) * 5,
        scratch_shapes=[
            pltpu.VMEM((8 * pairs, 4 * CHANNELS), jnp.bfloat16),
            pltpu.VMEM((4, pairs, CHANNELS), jnp.float32),
            pltpu.VMEM((pairs, CHANNELS), jnp.float32),
        ],
        compiler_params=PARAMS,
        name="correct",
    )(
        meta, *before, forward_guess[1], *ahead, adjoint_guess[0], before_slab, own_slab,
        weights, flipped, bias,
    )

    terms = over_all(residual).astype(jnp.float32)
    ahead_slab, error_slab = chain(False, terms, flipped, slopes)

    scale = STEP_SIZE / (row_count * zs * cols)
    grad_rows = 9 * CHANNELS + CHANNELS
    adjoints, grads = pl.pallas_call(
        functools.partial(finish_kernel, scale),
        out_shape=(shape_of(2, row_count, cols, CHANNELS), shape_of(grad_rows, CHANNELS)),
        in_specs=[VMEM] * 10,
        out_specs=(VMEM, VMEM),
        scratch_shapes=[
            pltpu.VMEM((6 * pairs, 4 * CHANNELS), jnp.bfloat16),
            pltpu.VMEM((4, pairs, CHANNELS), jnp.float32),
        ],
        compiler_params=PARAMS,
        name="finish",
    )(
        *ahead, adjoint_guess[0], ahead_slab, error_slab, even_taps, odd_taps, odd_slope, flipped
    )

    share = grads.reshape(depth, grad_rows // depth, CHANNELS)
    share = lax.all_to_all(share, "depth", 0, 0, tiled=True).sum(0)
    parts = [share] + [
        lax.ppermute(share, "rows", [(z, z ^ turn) for z in range(zs)]) for turn in range(1, zs)
    ]
    while len(parts) > 1:
        parts = [a + b for a, b in zip(parts[::2], parts[1::2])]
    share = parts[0]
    share = jnp.broadcast_to(share[None], (depth,) + share.shape)
    grads = lax.all_to_all(share, "depth", 0, 0, tiled=True).reshape(grad_rows, CHANNELS)
    grad_kernel = grads[: 9 * CHANNELS].reshape(3, 3, CHANNELS, CHANNELS)
    return states, adjoints, grad_kernel, grads[9 * CHANNELS]


def solution(mesh):
    placed = (
        P("rows", None, None),
        P("depth", "rows", None, None),
        P("depth", "rows", None, None),
        P("rows", None, None),
        P(),
        P(),
    )
    return jax.shard_map(
        shards,
        mesh=mesh,
        in_specs=placed,
        out_specs=(P("depth", "rows", None, None), P("depth", "rows", None, None), P(), P()),
        check_vma=False,
    )
```

```python
import functools

import jax
import jax.numpy as jnp
from jax import lax
from jax.experimental import pallas as pl
from jax.experimental.pallas import tpu as pltpu
from jax.sharding import Mesh, PartitionSpec as P

STEP_SIZE = 0.2
COARSE_SIZE = 2.0 * STEP_SIZE
CHUNK_SLABS = 8
AXES = ("depth", "rows")
CHANNELS = 128
SMEM = pl.BlockSpec(memory_space=pltpu.SMEM)
VMEM = pl.BlockSpec(memory_space=pltpu.VMEM)
PARAMS = pltpu.CompilerParams(vmem_limit_bytes=20 * 1024 * 1024)


def shape_of(*dims, dtype=jnp.float32):
    return jax.ShapeDtypeStruct(dims, dtype)


def spread(even, odd, width):
    count = even.shape[0]
    place = lax.broadcasted_iota(jnp.int32, even.shape, 0) % width
    before = jnp.where(place == 0, 0.0, pltpu.roll(odd, 1, 0))
    after = jnp.where(place == width - 1, 0.0, pltpu.roll(even, count - 1, 0))
    return jnp.concatenate([even, odd, before, after], axis=1).astype(jnp.bfloat16)


def taps(ref, start, count, width, weights):
    lhs = jnp.concatenate(
        [ref[start + tap * width : start + tap * width + count] for tap in range(3)], axis=1
    )
    return jnp.dot(lhs, weights, preferred_element_type=jnp.float32)


def halves(value):
    return value[:, :CHANNELS], value[:, CHANNELS:]


def pair_weights(kernel):
    none = jnp.zeros_like(kernel[:, 0])
    left, mid, right = kernel[:, 0], kernel[:, 1], kernel[:, 2]
    to_even = jnp.concatenate([mid, right, left, none], axis=1)
    to_odd = jnp.concatenate([left, mid, none, right], axis=1)
    return jnp.concatenate([to_even, to_odd], axis=2).reshape(12 * CHANNELS, 2 * CHANNELS)


def pack_weights(packed, pairs):
    packed[6 * CHANNELS :] = jnp.zeros((8 * CHANNELS, 2 * CHANNELS), packed.dtype)
    for tap in range(3):
        base = 4 * tap * CHANNELS
        packed[2 * tap * CHANNELS : 2 * (tap + 1) * CHANNELS] = pairs[base : base + 2 * CHANNELS]
        for plane in range(2):
            row = base + (2 + plane) * CHANNELS
            side = pairs[row : row + CHANNELS, plane * CHANNELS : (plane + 1) * CHANNELS]
            low = (6 + 4 * plane + tap) * CHANNELS
            packed[low : low + CHANNELS, :CHANNELS] = side
            packed[low + CHANNELS : low + 2 * CHANNELS, CHANNELS:] = side


def row_planes(ref, row, cols):
    return ref[row, pl.ds(0, cols // 2, stride=2), :], ref[row, pl.ds(1, cols // 2, stride=2), :]


def planes_of(refs_rows, cols):
    pairs = [row_planes(ref, row, cols) for ref, row in refs_rows]
    return jnp.concatenate([e for e, _ in pairs], 0), jnp.concatenate([o for _, o in pairs], 0)


def with_halo(top, main, bottom, halo):
    rows = [(top, 2 - halo + i) for i in range(halo)]
    rows += [(main, i) for i in range(main.shape[0])]
    return rows + [(bottom, i) for i in range(halo)]


def restricted(even, odd, pairs):
    both = even + odd
    return [
        (both[i * pairs : (i + 1) * pairs] + both[(i + 1) * pairs : (i + 2) * pairs]) * 0.25
        for i in range(0, both.shape[0] // pairs, 2)
    ]


def masked(value, pairs, at_top, at_bottom):
    count = value.shape[0] // pairs
    parts = [value[i * pairs : (i + 1) * pairs] for i in range(count)]
    parts[0] = jnp.where(at_top, jnp.zeros_like(parts[0]), parts[0])
    parts[-1] = jnp.where(at_bottom, jnp.zeros_like(parts[-1]), parts[-1])
    return jnp.concatenate(parts, 0)


def store_planes(out, scratch, rows, pairs):
    half = pairs // 2
    for i, row in enumerate(rows):
        scratch[...] = row
        for plane in range(2):
            base = (plane * len(rows) + i) * half
            out[base : base + half] = scratch[pl.ds(plane, half, stride=2), :]


def natural_rows(ref, scratch, count, pairs):
    half = pairs // 2
    rows = []
    for i in range(count):
        for plane in range(2):
            scratch[i, pl.ds(plane, half, stride=2), :] = ref[plane, i * half : (i + 1) * half]
        rows.append(scratch[i])
    return rows


def relax_kernel(
    shards_z, meta, top, main, bottom, first, weights, plain, bias, sent, fine, coarse, row, start
):
    pairs = main.shape[1] // 2
    at_top, at_bottom = meta[0] == 0, meta[0] == shards_z - 1
    even, odd = planes_of(with_halo(top, main, bottom, 2), main.shape[1])
    fine[...] = spread(jnp.tanh(even), jnp.tanh(odd), pairs)
    six = slice(pairs, 7 * pairs)
    conv_even, conv_odd = halves(taps(fine, 0, 6 * pairs, pairs, weights[...]))
    odd_even = masked(even[six] + STEP_SIZE * (conv_even + bias[...]), pairs, at_top, at_bottom)
    odd_odd = masked(odd[six] + STEP_SIZE * (conv_odd + bias[...]), pairs, at_top, at_bottom)
    fine[0 : 6 * pairs] = spread(jnp.tanh(odd_even), jnp.tanh(odd_odd), pairs)
    conv_even, conv_odd = halves(taps(fine, 0, 4 * pairs, pairs, weights[...]))
    four = slice(pairs, 5 * pairs)
    two_even = odd_even[four] + STEP_SIZE * (conv_even + bias[...])
    two_odd = odd_odd[four] + STEP_SIZE * (conv_odd + bias[...])
    fine_rows = restricted(two_even, two_odd, pairs)
    own = restricted(even, odd, pairs)
    place = lax.broadcasted_iota(jnp.int32, own[0].shape, 0)
    for i, value in enumerate(own):
        squashed = jnp.tanh(value)
        before = jnp.where(place == 0, 0.0, pltpu.roll(squashed, 1, 0))
        after = jnp.where(place == pairs - 1, 0.0, pltpu.roll(squashed, pairs - 1, 0))
        coarse[i * pairs : (i + 1) * pairs] = jnp.concatenate([before, squashed, after], 1).astype(
            jnp.bfloat16
        )
    conv = taps(coarse, 0, 2 * pairs, pairs, plain[...])
    rows = [
        fine_rows[i]
        - (own[i + 1] + COARSE_SIZE * (conv[i * pairs : (i + 1) * pairs] + bias[...]))
        for i in range(2)
    ]
    store_planes(sent, row, rows, pairs)
    even, odd = planes_of([(first, i) for i in range(4)], first.shape[1])
    store_planes(start, row, restricted(even, odd, pairs), pairs)
    share = sent.shape[0] - start.shape[0]
    sent[start.shape[0] :] = start[pl.ds(pl.multiple_of(meta[1] * share, share), share)]


def chain_kernel(forward, shards_z, chunk_slabs, meta, *refs):
    if forward:
        initial, terms, pairs, bias, around_out, own_out, *slopes, state, taps_in, weights = refs
    else:
        *slopes, terms, pairs, around_out, own_out, state, taps_in, weights = refs
    step, turns = pl.program_id(0), pl.num_programs(0)
    pos = meta[0]
    slab = own_out.shape[1]
    half = slab // 2
    cells = shards_z * slab

    @pl.when(step == 0)
    def _():
        state[...] = jnp.zeros_like(state)
        taps_in[...] = jnp.zeros_like(taps_in)
        pack_weights(weights, pairs)
        if forward:
            for turn in range(shards_z):
                state[:, half + turn * slab : half + (turn + 1) * slab] = initial[turn]

    mine = meta[1] if forward else turns - 1 - meta[1]

    @pl.when(step == mine)
    def _():
        around_out[...] = state[:, pl.ds(pl.multiple_of(pos * slab, half), 2 * slab)]

    chunk = chunk_slabs * slab
    for start in range(0, cells, chunk):
        span = slice(half + start, half + start + chunk)
        even, odd = state[0, span], state[1, span]
        if forward:
            even, odd = jnp.tanh(even), jnp.tanh(odd)
            slopes[0][0, start : start + chunk] = COARSE_SIZE * (1.0 - even * even)
            slopes[1][0, start : start + chunk] = COARSE_SIZE * (1.0 - odd * odd)
        taps_in[span] = spread(even, odd, half)
    for start in range(0, cells, chunk):
        own = jnp.concatenate(
            [taps_in[start + t * half : start + t * half + chunk, : 2 * CHANNELS] for t in range(3)],
            axis=1,
        )
        own = halves(
            jnp.dot(own, weights[: 6 * CHANNELS], preferred_element_type=jnp.float32)
        )
        sides = []
        for plane in range(2):
            lanes = slice((2 + plane) * CHANNELS, (3 + plane) * CHANNELS)
            columns = []
            for t in range(4):
                first = start + t * half
                columns.append(
                    jnp.concatenate(
                        [
                            taps_in[first + j * slab : first + j * slab + half, lanes]
                            for j in range(chunk_slabs)
                        ],
                        axis=0,
                    )
                )
            base = (6 + 4 * plane) * CHANNELS
            sides.append(
                jnp.dot(
                    jnp.concatenate(columns, axis=1),
                    weights[base : base + 4 * CHANNELS],
                    preferred_element_type=jnp.float32,
                )
            )
        for plane in range(2):
            for j in range(2 * chunk_slabs):
                low = start + j * half
                side = sides[plane][j // 2 * half : (j // 2 + 1) * half]
                part = own[plane][j * half : (j + 1) * half] + halves(side)[j % 2]
                if forward:
                    moved = COARSE_SIZE * (part + bias[...])
                else:
                    moved = slopes[plane][0, low : low + half] * part
                span = slice(half + low, half + low + half)
                first = plane * slab + j % 2 * half
                term = terms[0, low // slab, first : first + half]
                state[plane, span] = state[plane, span] + moved + term

    @pl.when(step == mine)
    def _():
        own_out[...] = state[:, pl.ds(pl.multiple_of(half + pos * slab, half), slab)]


def correct_kernel(
    shards_z,
    meta,
    before,
    guess,
    ahead_top,
    ahead_main,
    ahead_bottom,
    target,
    before_slab,
    own_slab,
    weights,
    flipped,
    bias,
    states,
    residual,
    even_taps,
    odd_taps,
    odd_slope,
    fine,
    natural,
    row,
):
    cols = before.shape[1]
    pairs = cols // 2
    at_top, at_bottom = meta[0] == 0, meta[0] == shards_z - 1
    even, odd = planes_of([(before, i) for i in range(8)], cols)
    rest = restricted(even, odd, pairs)
    found = natural_rows(before_slab, natural, 4, pairs)
    change = [jnp.where(meta[2] == 1, 0.0, a - b) for a, b in zip(found, rest)]
    change = jnp.concatenate([c for c in change for _ in range(2)], 0)
    even, odd = even + change, odd + change

    here, there = planes_of([(guess, i) for i in range(4)], cols)
    rest = restricted(here, there, pairs)
    found = natural_rows(own_slab, natural, 2, pairs)
    change = jnp.concatenate([a - b for a, b in zip(found, rest) for _ in range(2)], 0)
    here, there = here + change, there + change
    for i in range(4):
        span = slice(i * pairs, (i + 1) * pairs)
        states[1, i, pl.ds(0, pairs, stride=2), :] = here[span]
        states[1, i, pl.ds(1, pairs, stride=2), :] = there[span]

    tanh_even, tanh_odd = jnp.tanh(even), jnp.tanh(odd)
    fine[...] = spread(tanh_even, tanh_odd, pairs)
    six, four = slice(pairs, 7 * pairs), slice(pairs, 5 * pairs)
    even_taps[...] = fine[six]
    own = slice(2 * pairs, 6 * pairs)
    slope_even = STEP_SIZE * (1.0 - tanh_even[own] ** 2)
    slope_odd = STEP_SIZE * (1.0 - tanh_odd[own] ** 2)
    conv_even, conv_odd = halves(taps(fine, 0, 6 * pairs, pairs, weights[...]))
    even = masked(even[six] + STEP_SIZE * (conv_even + bias[...]), pairs, at_top, at_bottom)
    odd = masked(odd[six] + STEP_SIZE * (conv_odd + bias[...]), pairs, at_top, at_bottom)
    for i in range(4):
        span = slice((i + 1) * pairs, (i + 2) * pairs)
        states[0, i, pl.ds(0, pairs, stride=2), :] = even[span]
        states[0, i, pl.ds(1, pairs, stride=2), :] = odd[span]
    tanh_even, tanh_odd = jnp.tanh(even), jnp.tanh(odd)
    odd_taps[...] = spread(tanh_even, tanh_odd, pairs)
    step_even, step_odd = STEP_SIZE * (1.0 - tanh_even**2), STEP_SIZE * (1.0 - tanh_odd**2)
    odd_slope[0] = step_even[four]
    odd_slope[1] = step_odd[four]

    even, odd = planes_of(with_halo(ahead_top, ahead_main, ahead_bottom, 2), cols)
    fine[...] = spread(even, odd, pairs)
    conv_even, conv_odd = halves(taps(fine, 0, 6 * pairs, pairs, flipped[...]))
    even = masked(even[six] + step_even * conv_even, pairs, at_top, at_bottom)
    odd = masked(odd[six] + step_odd * conv_odd, pairs, at_top, at_bottom)
    fine[0 : 6 * pairs] = spread(even, odd, pairs)
    conv_even, conv_odd = halves(taps(fine, 0, 4 * pairs, pairs, flipped[...]))
    here, there = planes_of([(target, i) for i in range(4)], cols)
    even = even[four] + slope_even * conv_even - here
    odd = odd[four] + slope_odd * conv_odd - there
    store_planes(residual, row, restricted(even, odd, pairs), pairs)


def finish_kernel(
    scale,
    top,
    main,
    bottom,
    target,
    ahead_slab,
    own_slab,
    even_taps,
    odd_taps,
    odd_slope,
    flipped,
    adjoints,
    grads,
    fine,
    natural,
):
    cols = main.shape[1]
    pairs = cols // 2
    here, there = planes_of([(target, i) for i in range(4)], cols)
    change = natural_rows(own_slab, natural, 2, pairs)
    change = jnp.concatenate([c for c in change for _ in range(2)], 0)
    here, there = here + change, there + change
    for i in range(4):
        span = slice(i * pairs, (i + 1) * pairs)
        adjoints[0, i, pl.ds(0, pairs, stride=2), :] = here[span]
        adjoints[0, i, pl.ds(1, pairs, stride=2), :] = there[span]
    even, odd = planes_of(with_halo(top, main, bottom, 1), cols)
    found = natural_rows(ahead_slab, natural, 4, pairs)
    change = jnp.concatenate([found[0], found[1], found[1], found[2], found[2], found[3]], 0)
    even, odd = even + change, odd + change
    fine[...] = spread(even, odd, pairs)
    conv_even, conv_odd = halves(taps(fine, 0, 4 * pairs, pairs, flipped[...]))
    four = slice(pairs, 5 * pairs)
    even, odd = even[four], odd[four]
    new_even, new_odd = even + odd_slope[0] * conv_even, odd + odd_slope[1] * conv_odd
    for i in range(4):
        span = slice(i * pairs, (i + 1) * pairs)
        adjoints[1, i, pl.ds(0, pairs, stride=2), :] = new_even[span]
        adjoints[1, i, pl.ds(1, pairs, stride=2), :] = new_odd[span]
    right = jnp.concatenate(
        [
            jnp.concatenate([new_even, new_odd], 1).astype(jnp.bfloat16),
            jnp.concatenate([even, odd], 1).astype(jnp.bfloat16),
        ],
        0,
    )
    one, two, three, four_ = (slice(i * CHANNELS, (i + 1) * CHANNELS) for i in range(4))
    for tap in range(3):
        span = slice(tap * pairs, (tap + 4) * pairs)
        left = jnp.concatenate([even_taps[span], odd_taps[span]], 0)
        found = lax.dot_general(
            left, right, (((0,), (0,)), ((), ())), preferred_element_type=jnp.float32
        )
        base = tap * 3 * CHANNELS
        grads[base : base + CHANNELS] = scale * (found[one, two] + found[three, one])
        grads[base + CHANNELS : base + 2 * CHANNELS] = scale * (found[one, one] + found[two, two])
        grads[base + 2 * CHANNELS : base + 3 * CHANNELS] = scale * (
            found[two, one] + found[four_, two]
        )
    total = jnp.sum(new_even + new_odd + even + odd, axis=0, keepdims=True)
    base = 9 * CHANNELS
    rest = grads.shape[0] - base
    place = lax.broadcasted_iota(jnp.int32, (rest, CHANNELS), 0)
    grads[base:] = jnp.where(place == 0, scale * total, 0.0)


def shards(initial, forward_guess, adjoint_guess, cotangent, kernel, conv_bias):
    depth, zs = (lax.axis_size(axis) for axis in AXES)
    index, pos = (lax.axis_index(axis) for axis in AXES)
    at_first, at_last = index == 0, index == depth - 1
    row_count, cols, _ = initial.shape
    pairs = cols // 2
    slab = 2 * pairs // 2
    cells = zs * slab
    bias = conv_bias.reshape(1, CHANNELS)
    meta = jnp.stack([pos, index, at_first]).astype(jnp.int32)

    def moved(value, along, across):
        pairs_ = [
            (d * zs + z, (d + along) % depth * zs + z + across)
            for d in range(depth)
            for z in range(zs)
            if 0 <= z + across < zs
        ]
        return lax.ppermute(value, AXES, pairs_)

    main = jnp.where(at_last, initial, forward_guess[1])
    held = (moved(main[row_count - 2 :], 0, 1), main, moved(main[:2], 0, -1))
    target_sent = jnp.where(at_first, cotangent, adjoint_guess[0])

    weights = pair_weights(kernel)
    plain = kernel.reshape(9 * CHANNELS, CHANNELS)
    back_kernel = jnp.transpose(jnp.flip(kernel, (0, 1)), (0, 1, 3, 2))
    flipped = pair_weights(back_kernel)

    share = 2 * slab // depth
    sent = pl.pallas_call(
        functools.partial(relax_kernel, zs),
        out_shape=shape_of(2 * slab + share, CHANNELS),
        in_specs=[SMEM] + [VMEM] * 7,
        out_specs=VMEM,
        scratch_shapes=[
            pltpu.VMEM((8 * pairs, 4 * CHANNELS), jnp.bfloat16),
            pltpu.VMEM((4 * pairs, 3 * CHANNELS), jnp.bfloat16),
            pltpu.VMEM((pairs, CHANNELS), jnp.float32),
            pltpu.VMEM((2 * slab, CHANNELS), jnp.float32),
        ],
        compiler_params=PARAMS,
        name="relax",
    )(meta, *held, initial, weights, plain, bias)

    def over_rows(value):
        gathered = jnp.zeros((zs,) + value.shape, value.dtype)
        for turn in range(zs):
            place = lax.rem(pos + turn, zs)
            if turn:
                ring = [((i + turn) % zs, i) for i in range(zs)]
                part = lax.ppermute(value, "rows", ring)
            else:
                part = value
            gathered = lax.dynamic_update_slice_in_dim(gathered, part[None], place, 0)
        return gathered

    def over_all(value):
        return lax.all_gather(over_rows(value.astype(jnp.float16)), "depth")

    whole = lambda *dims: pl.BlockSpec(dims, lambda k: (0,) * len(dims))

    def chain(forward, terms, kernel_pairs, extra):
        term_at = (lambda k: lax.rem(k + depth - 1, depth)) if forward else (lambda k: depth - 1 - k)
        slope_at = (lambda k: k) if forward else term_at
        term_spec = pl.BlockSpec((1, zs) + terms.shape[2:], lambda k: (term_at(k), 0, 0, 0))
        slope_spec = pl.BlockSpec((1, cells, CHANNELS), lambda k: (slope_at(k), 0, 0))
        shapes = [shape_of(2, 2 * slab, CHANNELS), shape_of(2, slab, CHANNELS)]
        places = [whole(2, 2 * slab, CHANNELS), whole(2, slab, CHANNELS)]
        pair_spec = whole(*kernel_pairs.shape)
        if forward:
            operands = [meta, extra, terms, kernel_pairs, bias]
            specs = [SMEM, whole(*extra.shape), term_spec, pair_spec, whole(1, CHANNELS)]
            shapes += [shape_of(depth, cells, CHANNELS)] * 2
            places += [slope_spec] * 2
        else:
            operands = [meta, *extra, terms, kernel_pairs]
            specs = [SMEM, slope_spec, slope_spec, term_spec, pair_spec]
        return pl.pallas_call(
            functools.partial(chain_kernel, forward, zs, CHUNK_SLABS),
            grid=(depth,),
            out_shape=shapes,
            in_specs=specs,
            out_specs=places,
            scratch_shapes=[
                pltpu.VMEM((2, cells + slab, CHANNELS), jnp.float32),
                pltpu.VMEM((cells + slab, 4 * CHANNELS), jnp.bfloat16),
                pltpu.VMEM((14 * CHANNELS, 2 * CHANNELS), jnp.bfloat16),
            ],
            compiler_params=pltpu.CompilerParams(
                vmem_limit_bytes=24 * 1024 * 1024,
                allow_input_fusion=[operand is terms for operand in operands],
            ),
            name="forward_chain" if forward else "backward_chain",
        )(*operands)

    terms = over_all(sent)
    starts = jnp.swapaxes(terms[:, :, 2 * slab :], 0, 1).astype(jnp.float32)
    starts = starts.reshape(zs, 2, slab, CHANNELS)
    starts, held, target_sent = lax.optimization_barrier((starts, held, target_sent))
    before = moved(jnp.concatenate(held), 1, 0)
    ahead = (
        moved(target_sent[row_count - 2 :], -1, 1),
        moved(target_sent, -1, 0),
        moved(target_sent[:2], -1, -1),
    )
    before_slab, own_slab, *slopes = chain(
        True, terms.astype(jnp.float32), weights, starts
    )

    states, residual, even_taps, odd_taps, odd_slope = pl.pallas_call(
        functools.partial(correct_kernel, zs),
        out_shape=(
            shape_of(2, row_count, cols, CHANNELS),
            shape_of(2 * slab, CHANNELS),
            shape_of(6 * pairs, 4 * CHANNELS, dtype=jnp.bfloat16),
            shape_of(6 * pairs, 4 * CHANNELS, dtype=jnp.bfloat16),
            shape_of(2, 4 * pairs, CHANNELS),
        ),
        in_specs=[SMEM] + [VMEM] * 11,
        out_specs=(VMEM,) * 5,
        scratch_shapes=[
            pltpu.VMEM((8 * pairs, 4 * CHANNELS), jnp.bfloat16),
            pltpu.VMEM((4, pairs, CHANNELS), jnp.float32),
            pltpu.VMEM((pairs, CHANNELS), jnp.float32),
        ],
        compiler_params=PARAMS,
        name="correct",
    )(
        meta, before, forward_guess[1], *ahead, adjoint_guess[0], before_slab, own_slab,
        weights, flipped, bias,
    )

    terms = over_all(residual).astype(jnp.float32)
    ahead_slab, error_slab = chain(False, terms, flipped, slopes)

    scale = STEP_SIZE / (row_count * zs * cols)
    grad_rows = 9 * CHANNELS + CHANNELS
    adjoints, grads = pl.pallas_call(
        functools.partial(finish_kernel, scale),
        out_shape=(shape_of(2, row_count, cols, CHANNELS), shape_of(grad_rows, CHANNELS)),
        in_specs=[VMEM] * 10,
        out_specs=(VMEM, VMEM),
        scratch_shapes=[
            pltpu.VMEM((6 * pairs, 4 * CHANNELS), jnp.bfloat16),
            pltpu.VMEM((4, pairs, CHANNELS), jnp.float32),
        ],
        compiler_params=PARAMS,
        name="finish",
    )(
        *ahead, adjoint_guess[0], ahead_slab, error_slab, even_taps, odd_taps, odd_slope, flipped
    )

    share = grads.reshape(depth, grad_rows // depth, CHANNELS)
    share = lax.all_to_all(share, "depth", 0, 0, tiled=True).sum(0)
    parts = [share] + [
        lax.ppermute(share, "rows", [(z, z ^ turn) for z in range(zs)]) for turn in range(1, zs)
    ]
    while len(parts) > 1:
        parts = [a + b for a, b in zip(parts[::2], parts[1::2])]
    share = parts[0]
    share = jnp.broadcast_to(share[None], (depth,) + share.shape)
    grads = lax.all_to_all(share, "depth", 0, 0, tiled=True).reshape(grad_rows, CHANNELS)
    grad_kernel = grads[: 9 * CHANNELS].reshape(3, 3, CHANNELS, CHANNELS)
    return states, adjoints, grad_kernel, grads[9 * CHANNELS]


def solution(mesh):
    placed = (
        P("rows", None, None),
        P("depth", "rows", None, None),
        P("depth", "rows", None, None),
        P("rows", None, None),
        P(),
        P(),
    )
    return jax.shard_map(
        shards,
        mesh=mesh,
        in_specs=placed,
        out_specs=(P("depth", "rows", None, None), P("depth", "rows", None, None), P(), P()),
        check_vma=False,
    )
```
